32 devices in a mesh: seq: 16 (over z, x, core), res: 2 (over y).
Axes of the slice: x: 2, y: 2, z: 4, core: 2. Of those that a mesh axis runs over, the one named last changes fastest.
Arguments:
- embedded_aligned_rows: bfloat16 [48, 256, 768], P('seq', 'res'), may hold values from -12 to 12
- norm_multiplier: float32 [768], replicated, may hold values from 0.1 to 1.9
- asker_projector: bfloat16 [768, 768], replicated, may hold values from -1 to 1
- matcher_projector: bfloat16 [768, 768], replicated, may hold values from -1 to 1
- content_projector: bfloat16 [768, 768], replicated, may hold values from -0.21875 to 0.21875
- final_projector: bfloat16 [768, 768], replicated, may hold values from -0.21875 to 0.21875
Outputs:
- mixed: bfloat16 [48, 256, 768], P('seq', 'res')
The draws below stay inside these ranges and needn't reach their ends.
All inputs are finite; a program needn't handle non-finite values.
Results may differ from the reference program's by a relative error of at most 0.01.
Values may be sent and summed in bfloat16 or wider, within the bound.
No kernel may reach another device: no remote copies, remote signals or barrier semaphores. Data moves between devices by JAX's collectives and lax.ppermute only.
A program may use at most 64 MiB of HBM per device.

```python
import jax
import jax.numpy as jnp
from jax import lax

D = 768
HEADS = 12
SEQS = 48
RES = 256
N_SEQ = 16


def weight_pair(key):
    base = jax.random.normal(jax.random.fold_in(key, 21), (D, D), jnp.float32) / jnp.sqrt(jnp.float32(D))
    other = jax.random.normal(jax.random.fold_in(key, 22), (D, D), jnp.float32) / jnp.sqrt(jnp.float32(D))
    return (base, other)


def draw_asker_projector(key, part):
    base, other = weight_pair(key)
    return jnp.clip(base, -1.0, 1.0).astype(jnp.bfloat16)


def draw_matcher_projector(key, part):
    base, other = weight_pair(key)
    content_array = other
    return jnp.clip(content_array, -1.0, 1.0).astype(jnp.bfloat16)


def draw_embedded_aligned_rows(key, part):
    noise = jax.random.normal(jax.random.fold_in(key, 11), (SEQS, RES, D), jnp.float32)
    content_array = noise
    return jnp.clip(content_array, -12.0, 12.0).astype(jnp.bfloat16)


def scatter_about(rng, extent, scale, most, kind=jnp.bfloat16):
    return jnp.clip(scale * jax.random.normal(rng, extent, jnp.float32), -most, most).astype(kind)


def setup_inputs(seed: int = 0) -> dict:
    streams_of = jax.random.split(jax.random.key(seed), 7)
    return {
        "embedded_aligned_rows": draw_embedded_aligned_rows(jax.random.fold_in(streams_of[6], 71), 0),
        "norm_multiplier": jnp.clip(1.0 + 0.18 * jax.random.normal(streams_of[1], (D,), jnp.float32), 0.1, 1.9),
        "asker_projector": draw_asker_projector(jax.random.fold_in(streams_of[6], 71), 0),
        "matcher_projector": draw_matcher_projector(jax.random.fold_in(streams_of[6], 71), 0),
        "content_projector": scatter_about(streams_of[4], (D, D), D ** -0.5, 0.21875),
        "final_projector": scatter_about(streams_of[5], (D, D), D ** -0.5, 0.21875),
    }


def standardize_rows(embedded_aligned_rows, norm_multiplier):
    content_array = embedded_aligned_rows.astype(jnp.float32)
    center = content_array - lax.optimization_barrier(jnp.mean(content_array, axis=-1, keepdims=True))
    spread = lax.optimization_barrier(jnp.mean(center * center, axis=-1, keepdims=True))
    return (center / jnp.sqrt(spread + 1e-05) * norm_multiplier).astype(jnp.bfloat16)

def reference(embedded_aligned_rows, norm_multiplier, asker_projector, matcher_projector, content_projector, final_projector):
    element_number, overall_span, embedding_dimension = embedded_aligned_rows.shape
    heads = HEADS
    hsize = embedding_dimension // heads
    tile_group = embedded_aligned_rows.reshape(N_SEQ, element_number // N_SEQ, overall_span, embedding_dimension)
    scale = 1.0 / (jnp.sqrt(jnp.float32(hsize)) * jnp.sqrt(jnp.float32(element_number)))

    def project(normed, weight):
        rows = normed.reshape(-1, embedding_dimension)
        out = jnp.dot(rows, weight, preferred_element_type=jnp.float32).astype(jnp.bfloat16)
        return out.reshape(normed.shape[0], overall_span, heads, hsize)

    def add_logits(total, block):
        normed = standardize_rows(block, norm_multiplier)
        query = project(normed, asker_projector).astype(jnp.float32)
        keys = project(normed, matcher_projector).astype(jnp.float32)
        return (total + jnp.einsum('sihe,sjhe->hij', query, keys), None)
    start = jnp.zeros((heads, overall_span, overall_span), jnp.float32)
    logits, _ = lax.scan(add_logits, start, tile_group)
    probs = jax.nn.softmax(logits * scale, axis=-1).astype(jnp.bfloat16)
    weights = probs.astype(jnp.float32)

    def mix_block(carry, block):
        normed = standardize_rows(block, norm_multiplier)
        value = project(normed, content_projector).astype(jnp.float32)
        attended = jnp.einsum('hij,sjhe->sihe', weights, value).astype(jnp.bfloat16)
        rows = attended.reshape(-1, embedding_dimension)
        mixed = jnp.dot(rows, final_projector, preferred_element_type=jnp.float32).astype(jnp.bfloat16)
        return (carry, mixed.reshape(block.shape))
    _, mixed = lax.scan(mix_block, jnp.zeros((), jnp.float32), tile_group)
    return mixed.reshape(element_number, overall_span, embedding_dimension)
```

```python
import functools

import jax
import jax.numpy as jnp
from jax import lax
from jax.experimental import pallas as pl
from jax.experimental.pallas import tpu as pltpu
from jax.sharding import PartitionSpec as P

HEADS = 12
LANES = 128
CORES = 2

VMEM = pl.BlockSpec(memory_space=pltpu.VMEM)
SMEM = pl.BlockSpec(memory_space=pltpu.SMEM)
PARAMS = pltpu.CompilerParams(vmem_limit_bytes=48 << 20)


def standardize(x, gain):
    x = x.astype(jnp.float32)
    center = x - jnp.mean(x, axis=-1, keepdims=True)
    spread = jnp.mean(center * center, axis=-1, keepdims=True)
    return (center * (1.0 / jnp.sqrt(spread + 1e-05)) * gain).astype(jnp.bfloat16)


def rows_of(x_ref, gain_ref):
    s, r, d = x_ref.shape
    return standardize(x_ref[...].reshape(s * r, d), gain_ref[...])


def project(rows, w_ref):
    return jnp.dot(rows, w_ref[...], preferred_element_type=jnp.float32).astype(jnp.bfloat16)


def lane_group(y, s, r, group):
    return jnp.concatenate(
        [y[i * r : (i + 1) * r, group * LANES : (group + 1) * LANES] for i in range(s)], axis=1
    )


def write_scores(core, q_ref, k_ref, send_ref, keep_ref):
    groups, packed, _ = q_ref.shape
    blocks, heads, share, cols = keep_ref.shape
    per_core = groups // CORES
    pack = heads // per_core
    r = packed // pack
    for out_ref, side in ((send_ref, 1 - core), (keep_ref, core)):
        for t in range(per_core):
            g = side * per_core + t
            part = lax.dot_general(
                q_ref[g], k_ref[g], (((1,), (1,)), ((), ())), preferred_element_type=jnp.float32
            )
            for h in range(pack):
                out_ref[:, t * pack + h] = part[h * r : (h + 1) * r].reshape(blocks, share, cols)


def own_kernel(ids, x_ref, gain_ref, wq_ref, wk_ref, q_ref, send_ref, keep_ref, k_scr):
    s, r, d = x_ref.shape
    groups = d // LANES
    hsize = d // HEADS
    rows = rows_of(x_ref, gain_ref)
    q = project(rows, wq_ref)
    k = project(rows, wk_ref)
    lane = lax.broadcasted_iota(jnp.int32, (r, s * LANES), 1) % LANES // hsize
    for g in range(groups):
        k_scr[g] = lane_group(k, s, r, g)
        both = lane_group(q, s, r, g)
        for h in range(LANES // hsize):
            q_ref[g, h * r : (h + 1) * r] = jnp.where(lane == h, both, jnp.zeros_like(both))
    write_scores(ids[0], q_ref, k_scr, send_ref, keep_ref)


def other_kernel(ids, x_ref, gain_ref, wk_ref, q_ref, send_ref, keep_ref, k_scr):
    s, r, d = x_ref.shape
    k = project(rows_of(x_ref, gain_ref), wk_ref)
    for g in range(d // LANES):
        k_scr[g] = lane_group(k, s, r, g)
    write_scores(ids[0], q_ref, k_scr, send_ref, keep_ref)


def value_kernel(x_ref, gain_ref, wv_ref, v_ref):
    s, r, d = x_ref.shape
    v = project(rows_of(x_ref, gain_ref), wv_ref)
    for g in range(d // LANES):
        v_ref[g] = lane_group(v, s, r, g)


def merge_kernel(n, *refs):
    keep, got, out_ref = refs[:n], refs[n : 2 * n], refs[2 * n]
    for h in range(out_ref.shape[1]):
        total = jnp.concatenate([a[:, h] + b[:, h] for a, b in zip(keep, got)], axis=-1)
        total = total - jnp.max(total, axis=-1, keepdims=True)
        out_ref[:, h] = total.astype(out_ref.dtype)


def softmax_kernel(scale, parts_ref, out_ref):
    blocks = parts_ref.shape[0]
    for h in range(parts_ref.shape[1]):
        logits = jnp.sum(parts_ref[:, h].astype(jnp.float32), axis=0) * scale
        p = jnp.exp(logits - jnp.max(logits, axis=-1, keepdims=True))
        p = (p / jnp.sum(p, axis=-1, keepdims=True)).astype(out_ref.dtype)
        for b in range(blocks):
            out_ref[b, h] = p


def mix_kernel(n, ids, *refs):
    mine_ref, got_ref = refs[:2]
    v_refs = refs[2 : 2 + n]
    wf_ref, out_ref, att_scr = refs[2 + n :]
    s, r, d = out_ref.shape
    groups = d // LANES
    hsize = d // HEADS
    pack = LANES // hsize
    blocks, heads, share, cols = mine_ref.shape
    per_core = groups // CORES
    lane = lax.broadcasted_iota(jnp.int32, (r, s * LANES), 1) % LANES // hsize
    for p_ref, side in ((mine_ref, ids[0]), (got_ref, 1 - ids[0])):
        for t in range(per_core):
            g = side * per_core + t
            p = jnp.concatenate(
                [p_ref[:, t * pack + h].reshape(r, cols) for h in range(pack)], axis=0
            )
            v = jnp.concatenate([v_ref[g] for v_ref in v_refs], axis=0)
            both = jnp.dot(p, v, preferred_element_type=jnp.float32)
            got = both[:r]
            for h in range(1, pack):
                got = jnp.where(lane == h, both[h * r : (h + 1) * r], got)
            att_scr[g] = got.astype(jnp.bfloat16)
    rows = jnp.concatenate(
        [
            jnp.concatenate(
                [att_scr[g, :, i * LANES : (i + 1) * LANES] for g in range(groups)], axis=1
            )
            for i in range(s)
        ],
        axis=0,
    )
    mixed = jnp.dot(rows, wf_ref[...], preferred_element_type=jnp.float32)
    out_ref[...] = mixed.astype(out_ref.dtype).reshape(s, r, d)


def call(kernel, out_shape, args, ids=None, scratch=(), flops=0, name=None):
    ins = ((ids,) if ids is not None else ()) + tuple(args)
    specs = ([SMEM] if ids is not None else []) + [VMEM] * len(args)
    moved = sum(a.size * a.dtype.itemsize for a in args)
    return pl.pallas_call(
        kernel,
        out_shape=out_shape,
        in_specs=specs,
        out_specs=jax.tree.map(lambda _: VMEM, out_shape),
        scratch_shapes=list(scratch),
        compiler_params=PARAMS,
        cost_estimate=pl.CostEstimate(flops=flops, bytes_accessed=moved, transcendentals=0),
        name=name,
    )(*ins)


def body(n_seq, n_res, x, gain, wq, wk, wv, wf):
    s, r, d = x.shape
    groups = d // LANES
    hsize = d // HEADS
    pack = LANES // hsize
    blocks = n_seq // CORES
    share = r // blocks
    heads = HEADS // CORES
    f32, bf16 = jnp.float32, jnp.bfloat16
    shape = jax.ShapeDtypeStruct

    gain = gain.reshape(1, d)
    core = lax.axis_index("seq") % CORES
    ids = core.astype(jnp.int32).reshape(1)
    swap = [(i, i ^ 1) for i in range(n_seq)]
    peers = [[b * CORES + c for b in range(blocks)] for c in range(CORES)]

    def exchange(y):
        return lax.all_to_all(y, "seq", 0, 0, tiled=True, axis_index_groups=peers)

    others = [
        lax.ppermute(x, "res", [(i, (i + k) % n_res) for i in range(n_res)])
        for k in range(1, n_res)
    ]
    part = shape((blocks, heads, share, r), f32)
    dots = 2 * s * r * d
    q, send, keep = call(
        own_kernel,
        (shape((groups, pack * r, s * LANES), bf16), part, part),
        (x, gain, wq, wk),
        ids,
        scratch=[pltpu.VMEM((groups, r, s * LANES), bf16)],
        flops=dots * (2 * d + r),
        name="own_scores",
    )
    keeps, gots = [keep], [lax.ppermute(send, "seq", swap)]
    for other in others:
        send, keep = call(
            other_kernel,
            (part, part),
            (other, gain, wk, q),
            ids,
            scratch=[pltpu.VMEM((groups, r, s * LANES), bf16)],
            flops=dots * (d + r),
            name="other_scores",
        )
        keeps.append(keep)
        gots.append(lax.ppermute(send, "seq", swap))
    values = [
        call(
            value_kernel,
            shape((groups, r, s * LANES), bf16),
            (block, gain, wv),
            flops=dots * d,
            name="values",
        )
        for block in [x] + others
    ]
    cols = r * n_res
    pieces = shape((blocks, heads, share, cols), bf16)
    partial = call(
        functools.partial(merge_kernel, n_res), pieces, (*keeps, *gots), name="merge_scores"
    )
    scale = float(hsize * s * n_seq) ** -0.5
    probs = call(
        functools.partial(softmax_kernel, scale), pieces, (exchange(partial),), name="softmax"
    )
    mine = exchange(probs)
    got = lax.ppermute(mine, "seq", swap)
    return call(
        functools.partial(mix_kernel, n_res),
        shape((s, r, d), bf16),
        (mine, got, *values, wf),
        ids,
        scratch=[pltpu.VMEM((groups, r, s * LANES), bf16)],
        flops=dots * (d + cols),
        name="mix",
    )


def solution(mesh):
    placed = (P("seq", "res", None), P(), P(), P(), P(), P())
    return jax.shard_map(
        functools.partial(body, mesh.shape["seq"], mesh.shape["res"]),
        mesh=mesh,
        in_specs=placed,
        out_specs=P("seq", "res", None),
        check_vma=False,
    )
```

```python
import functools

import jax
import jax.numpy as jnp
from jax import lax
from jax.experimental import pallas as pl
from jax.experimental.pallas import tpu as pltpu
from jax.sharding import PartitionSpec as P

HEADS = 12
LANES = 128
CORES = 2


VMEM = pl.BlockSpec(memory_space=pltpu.VMEM)
SMEM = pl.BlockSpec(memory_space=pltpu.SMEM)
ANY = pl.BlockSpec(memory_space=pl.ANY)
PARAMS = pltpu.CompilerParams(vmem_limit_bytes=48 << 20)


def standardize(x, gain):
    x = x.astype(jnp.float32)
    center = x - jnp.mean(x, axis=-1, keepdims=True)
    spread = jnp.mean(center * center, axis=-1, keepdims=True)
    return (center * (1.0 / jnp.sqrt(spread + 1e-05)) * gain).astype(jnp.bfloat16)


def rows_of(x_ref, gain_ref):
    s, r, d = x_ref.shape
    return standardize(x_ref[...].reshape(s * r, d), gain_ref[...])


def project(rows, w_ref):
    return jnp.dot(rows, w_ref[...], preferred_element_type=jnp.float32).astype(jnp.bfloat16)


def lane_group(y, s, r, group):
    return jnp.concatenate(
        [y[i * r : (i + 1) * r, group * LANES : (group + 1) * LANES] for i in range(s)], axis=1
    )


def write_scores(core, q_ref, k_ref, send_ref, keep_ref):
    groups, packed, _ = q_ref.shape
    blocks, heads, share, cols = keep_ref.shape
    per_core = groups // CORES
    pack = heads // per_core
    r = packed // pack
    for out_ref, side in ((send_ref, 1 - core), (keep_ref, core)):
        for t in range(per_core):
            g = side * per_core + t
            part = lax.dot_general(
                q_ref[g], k_ref[g], (((1,), (1,)), ((), ())), preferred_element_type=jnp.float32
            )
            for h in range(pack):
                out_ref[:, t * pack + h] = part[h * r : (h + 1) * r].reshape(blocks, share, cols)


def own_kernel(
    ids, x_ref, gain_ref, wq_ref, wk_ref, wv_ref, q_ref, send_ref, keep_ref, v_ref, k_scr
):
    s, r, d = x_ref.shape
    hsize = d // HEADS
    rows = rows_of(x_ref, gain_ref)
    q = project(rows, wq_ref)
    k = project(rows, wk_ref)
    lane = lax.broadcasted_iota(jnp.int32, (r, s * LANES), 1) % LANES // hsize
    for g in range(d // LANES):
        k_scr[g] = lane_group(k, s, r, g)
        both = lane_group(q, s, r, g)
        for h in range(LANES // hsize):
            q_ref[g, h * r : (h + 1) * r] = jnp.where(lane == h, both, jnp.zeros_like(both))
    write_scores(ids[0], q_ref, k_scr, send_ref, keep_ref)
    v = project(rows, wv_ref)
    for g in range(d // LANES):
        v_ref[g] = lane_group(v, s, r, g)


def other_kernel(ids, x_ref, gain_ref, wk_ref, q_ref, send_ref, keep_ref, k_scr):
    s, r, d = x_ref.shape
    k = project(rows_of(x_ref, gain_ref), wk_ref)
    for g in range(d // LANES):
        k_scr[g] = lane_group(k, s, r, g)
    write_scores(ids[0], q_ref, k_scr, send_ref, keep_ref)


def value_kernel(x_ref, gain_ref, wv_ref, after_ref, v_ref):
    s, r, d = x_ref.shape
    v = project(rows_of(x_ref, gain_ref), wv_ref)
    for g in range(d // LANES):
        v_ref[g] = lane_group(v, s, r, g)


def merge_kernel(n, ids, *refs):
    keep, got, outs = refs[:n], refs[n : 2 * n], refs[2 * n + n - 1 :]
    for k, out_ref in enumerate(outs):
        b = ids[1] ^ k
        for h in range(out_ref.shape[0]):
            total = jnp.concatenate([x[b, h] + y[b, h] for x, y in zip(keep, got)], axis=-1)
            total = total - jnp.max(total, axis=-1, keepdims=True)
            out_ref[h] = total.astype(out_ref.dtype)


def sum_kernel(own_ref, *refs):
    parts, total_ref, sent_ref = refs[:-2], refs[-2], refs[-1]
    for h in range(own_ref.shape[0]):
        total = own_ref[h]
        for part in parts:
            total = total + part[h].astype(jnp.float32)
        total_ref[h] = total
        sent_ref[h] = total.astype(sent_ref.dtype)


def softmax_kernel(scale, total_ref, got_ref, out_ref):
    for h in range(out_ref.shape[0]):
        logits = (total_ref[h] + got_ref[h].astype(jnp.float32)) * scale
        p = jnp.exp(logits - jnp.max(logits, axis=-1, keepdims=True))
        out_ref[h] = (p / jnp.sum(p, axis=-1, keepdims=True)).astype(out_ref.dtype)


def attend(p_refs, v_refs, side, hsize, put):
    heads, share, _ = p_refs[0].shape
    pack = LANES // hsize
    r = share * len(p_refs)
    per_core = heads // pack
    width = v_refs[0].shape[-1]
    lane = lax.broadcasted_iota(jnp.int32, (r, width), 1) % LANES // hsize
    for t in range(per_core):
        g = side * per_core + t
        p = jnp.concatenate(
            [p_ref[t * pack + h] for h in range(pack) for p_ref in p_refs], axis=0
        )
        v = jnp.concatenate([v_ref[g] for v_ref in v_refs], axis=0)
        both = jnp.dot(p, v, preferred_element_type=jnp.float32)
        got = both[:r]
        for h in range(1, pack):
            got = jnp.where(lane == h, both[h * r : (h + 1) * r], got)
        put(t, got.astype(jnp.bfloat16))


def attend_kernel(n_p, n_v, hsize, ids, *refs):
    p_refs, v_refs, out_ref = refs[:n_p], refs[n_p : n_p + n_v], refs[-1]

    def put(t, rows):
        out_ref[t] = rows

    attend(p_refs, v_refs, ids[0], hsize, put)


def mix_kernel(n_p, n_v, ids, *refs):
    p_refs, v_refs = refs[:n_p], refs[n_p : n_p + n_v]
    mine_ref, wf_ref, out_ref, att_scr = refs[n_p + n_v :]
    s, r, d = out_ref.shape
    share = r // n_p
    groups = d // LANES
    per_core = groups // CORES
    core = ids[0]
    for t in range(per_core):
        att_scr[core * per_core + t] = mine_ref[t]

    def put(t, rows):
        att_scr[(1 - core) * per_core + t] = rows

    attend(p_refs, v_refs, 1 - core, d // HEADS, put)
    rows = jnp.concatenate(
        [
            jnp.concatenate(
                [att_scr[g, :, i * LANES : (i + 1) * LANES] for g in range(groups)], axis=1
            )
            for i in range(s)
        ],
        axis=0,
    )
    mixed = jnp.dot(rows, wf_ref[...], preferred_element_type=jnp.float32).astype(out_ref.dtype)
    for i in range(s):
        for k in range(n_p):
            start = pl.multiple_of((ids[1] ^ k) * share, share)
            out_ref[i, pl.ds(start, share)] = mixed[i * r + k * share : i * r + (k + 1) * share]


def call(kernel, out_shape, args, ids=None, order=(), scratch=(), flops=0, name=None):
    ins = ((ids,) if ids is not None else ()) + tuple(args) + tuple(order)
    specs = ([SMEM] if ids is not None else []) + [VMEM] * len(args) + [ANY] * len(order)
    moved = sum(a.size * a.dtype.itemsize for a in args)
    return pl.pallas_call(
        kernel,
        out_shape=out_shape,
        in_specs=specs,
        out_specs=jax.tree.map(lambda _: VMEM, out_shape),
        scratch_shapes=list(scratch),
        compiler_params=PARAMS,
        cost_estimate=pl.CostEstimate(flops=flops, bytes_accessed=moved, transcendentals=0),
        name=name,
    )(*ins)


def body(n_seq, n_res, x, gain, wq, wk, wv, wf):
    s, r, d = x.shape
    groups = d // LANES
    hsize = d // HEADS
    pack = LANES // hsize
    heads = HEADS // CORES
    blocks = n_seq // CORES
    inner = blocks // 2
    share = r // inner
    cols = r * n_res
    f32, bf16 = jnp.float32, jnp.bfloat16
    shape = jax.ShapeDtypeStruct

    gain = gain.reshape(1, d)
    place = lax.axis_index("seq")
    ids = jnp.stack([place & 1, (place >> 1) & (inner - 1)]).astype(jnp.int32)

    def hop(y, k):
        return lax.ppermute(y, "seq", [(i, i ^ k) for i in range(n_seq)])

    others = [
        lax.ppermute(x, "res", [(i, (i + k) % n_res) for i in range(n_res)])
        for k in range(1, n_res)
    ]
    part = shape((inner, heads, share, r), f32)
    grouped = shape((groups, r, s * LANES), bf16)
    scratch = [pltpu.VMEM(grouped.shape, bf16)]
    dots = 2 * s * r * d
    q, send, keep, value = call(
        own_kernel,
        (shape((groups, pack * r, s * LANES), bf16), part, part, grouped),
        (x, gain, wq, wk, wv),
        ids,
        scratch=scratch,
        flops=dots * (3 * d + r),
        name="own_scores",
    )
    keeps, gots, values = [keep], [hop(send, 1)], [value]
    for other in others:
        send, keep = call(
            other_kernel,
            (part, part),
            (other, gain, wk, q),
            ids,
            scratch=scratch,
            flops=dots * (d + r),
            name="other_scores",
        )
        keeps.append(keep)
        gots.append(hop(send, 1))
    for other in others:
        values.append(
            call(
                value_kernel,
                grouped,
                (other, gain, wv),
                order=(keeps[-1],),
                flops=dots * d,
                name="values",
            )
        )
    piece = shape((heads, share, cols), bf16)
    total = shape((heads, share, cols), f32)
    own, *sent = call(
        functools.partial(merge_kernel, n_res),
        (total, *[piece] * (inner - 1)),
        (*keeps, *gots),
        ids,
        order=values[1:],
        name="merge_scores",
    )
    parts = [hop(y, CORES * (k + 1)) for k, y in enumerate(sent)]
    half, sent = call(sum_kernel, (total, piece), (own, *parts), name="sum_scores")
    scale = float(hsize * s * n_seq) ** -0.5
    probs = call(
        functools.partial(softmax_kernel, scale),
        piece,
        (half, hop(sent, CORES * inner)),
        name="softmax",
    )
    mine = [probs] + [hop(probs, CORES * k) for k in range(1, inner)]
    got = [hop(y, 1) for y in mine]
    attended = call(
        functools.partial(attend_kernel, inner, n_res, hsize),
        shape((groups // CORES, r, s * LANES), bf16),
        (*mine, *values),
        ids,
        flops=dots * cols,
        name="attend_mine",
    )
    return call(
        functools.partial(mix_kernel, inner, n_res),
        shape((s, r, d), bf16),
        (*got, *values, attended, wf),
        ids,
        scratch=scratch,
        flops=dots * (d + cols),
        name="mix",
    )


def solution(mesh):
    placed = (P("seq", "res", None), P(), P(), P(), P(), P())
    return jax.shard_map(
        functools.partial(body, mesh.shape["seq"], mesh.shape["res"]),
        mesh=mesh,
        in_specs=placed,
        out_specs=P("seq", "res", None),
        check_vma=False,
    )
```

```python
import functools

import jax
import jax.numpy as jnp
from jax import lax
from jax.experimental import pallas as pl
from jax.experimental.pallas import tpu as pltpu
from jax.sharding import PartitionSpec as P

HEADS = 12
LANES = 128
CORES = 2


VMEM = pl.BlockSpec(memory_space=pltpu.VMEM)
SMEM = pl.BlockSpec(memory_space=pltpu.SMEM)
ANY = pl.BlockSpec(memory_space=pl.ANY)
HBM = pl.BlockSpec(memory_space=pltpu.HBM)
PARAMS = pltpu.CompilerParams(vmem_limit_bytes=48 << 20)


def standardize(x, gain):
    x = x.astype(jnp.float32)
    center = x - jnp.mean(x, axis=-1, keepdims=True)
    spread = jnp.mean(center * center, axis=-1, keepdims=True)
    return (center * (1.0 / jnp.sqrt(spread + 1e-05)) * gain).astype(jnp.bfloat16)


def rows_of(x_ref, gain_ref):
    s, r, d = x_ref.shape
    return standardize(x_ref[...].reshape(s * r, d), gain_ref[...].reshape(1, d))


def project(rows, w_ref):
    return jnp.dot(rows, w_ref[...], preferred_element_type=jnp.float32).astype(jnp.bfloat16)


def lane_group(y, s, r, group):
    return jnp.concatenate(
        [y[i * r : (i + 1) * r, group * LANES : (group + 1) * LANES] for i in range(s)], axis=1
    )


def write_scores(q_ref, q_at, k_ref, k_at, out_ref):
    blocks, heads, share, cols = out_ref.shape
    per_core = q_ref.shape[0] // CORES
    pack = heads // per_core
    r = blocks * share
    for t in range(per_core):
        part = lax.dot_general(
            q_ref[q_at + t],
            k_ref[k_at + t],
            (((1,), (1,)), ((), ())),
            preferred_element_type=jnp.float32,
        )
        for h in range(pack):
            out_ref[:, t * pack + h] = part[h * r : (h + 1) * r].reshape(blocks, share, cols)


def own_kernel(
    ids, gain_ref, x_hbm, wq_hbm, wk_hbm, q_ref, send_ref, keep_ref, x_ref, wq_ref, wk_ref, k_scr, sems
):
    copies = [
        pltpu.make_async_copy(src, dst, sems.at[i])
        for i, (src, dst) in enumerate(((x_hbm, x_ref), (wk_hbm, wk_ref), (wq_hbm, wq_ref)))
    ]
    for copy in copies:
        copy.start()
    s, r, d = x_ref.shape
    hsize = d // HEADS
    per_core = d // LANES // CORES
    copies[0].wait()
    rows = rows_of(x_ref, gain_ref)
    copies[1].wait()
    k = project(rows, wk_ref)
    for g in range(d // LANES):
        k_scr[g] = lane_group(k, s, r, g)
    copies[2].wait()
    q = project(rows, wq_ref)
    lane = lax.broadcasted_iota(jnp.int32, (r, s * LANES), 1) % LANES // hsize
    for g in range(d // LANES):
        both = lane_group(q, s, r, g)
        for h in range(LANES // hsize):
            q_ref[g, h * r : (h + 1) * r] = jnp.where(lane == h, both, jnp.zeros_like(both))
    for out_ref, side in ((send_ref, 1 - ids[0]), (keep_ref, ids[0])):
        write_scores(q_ref, side * per_core, k_scr, side * per_core, out_ref)


def send_kernel(ids, x_ref, gain_ref, wk_ref, q_ref, after_ref, send_ref, kept_ref, k_scr):
    s, r, d = x_ref.shape
    per_core = d // LANES // CORES
    k = project(rows_of(x_ref, gain_ref), wk_ref)
    for g in range(d // LANES):
        k_scr[g] = lane_group(k, s, r, g)
    write_scores(q_ref, (1 - ids[0]) * per_core, k_scr, (1 - ids[0]) * per_core, send_ref)
    for t in range(per_core):
        kept_ref[t] = k_scr[ids[0] * per_core + t]


def keep_kernel(ids, kept_ref, q_ref, after_ref, keep_ref):
    write_scores(q_ref, ids[0] * kept_ref.shape[0], kept_ref, 0, keep_ref)


def value_kernel(x_ref, gain_ref, wv_ref, after_ref, v_ref):
    s, r, d = x_ref.shape
    v = project(rows_of(x_ref, gain_ref), wv_ref)
    for g in range(d // LANES):
        v_ref[g] = lane_group(v, s, r, g)


def merge_kernel(ids, keep_ref, got_ref, *refs):
    outs = refs[-keep_ref.shape[0] :]
    for k, out_ref in enumerate(outs):
        b = ids[1] ^ k
        out_ref[...] = keep_ref[b] + got_ref[b]


def sum_kernel(*refs):
    total = refs[0][...]
    for part in refs[1:-1]:
        total = total + part[...]
    refs[-1][...] = total


def softmax_kernel(scale, n, *refs):
    halves, gots, out_ref = refs[:n], refs[n : 2 * n], refs[2 * n]
    logits = jnp.concatenate([a[...] + b[...] for a, b in zip(halves, gots)], axis=-1) * scale
    p = jnp.exp(logits - jnp.max(logits, axis=-1, keepdims=True))
    out_ref[...] = (p / jnp.sum(p, axis=-1, keepdims=True)).astype(out_ref.dtype)


def attend(p_refs, v_refs, side, hsize, put):
    heads, share, _ = p_refs[0].shape
    pack = LANES // hsize
    r = share * len(p_refs)
    per_core = heads // pack
    width = v_refs[0].shape[-1]
    lane = lax.broadcasted_iota(jnp.int32, (r, width), 1) % LANES // hsize
    for t in range(per_core):
        g = side * per_core + t
        p = jnp.concatenate(
            [p_ref[t * pack + h] for h in range(pack) for p_ref in p_refs], axis=0
        )
        v = jnp.concatenate([v_ref[g] for v_ref in v_refs], axis=0)
        both = jnp.dot(p, v, preferred_element_type=jnp.float32)
        got = both[:r]
        for h in range(1, pack):
            got = jnp.where(lane == h, both[h * r : (h + 1) * r], got)
        put(t, got.astype(jnp.bfloat16))


def attend_kernel(n_p, n_v, hsize, ids, *refs):
    p_refs, v_refs, out_ref = refs[:n_p], refs[n_p : n_p + n_v], refs[-1]

    def put(t, rows):
        out_ref[t] = rows

    attend(p_refs, v_refs, ids[0], hsize, put)


def mix_kernel(n_p, n_v, ids, *refs):
    p_refs, v_refs = refs[:n_p], refs[n_p : n_p + n_v]
    mine_ref, wf_ref, out_ref, att_scr = refs[n_p + n_v :]
    s, r, d = out_ref.shape
    share = r // n_p
    groups = d // LANES
    per_core = groups // CORES
    core = ids[0]
    for t in range(per_core):
        att_scr[core * per_core + t] = mine_ref[t]

    def put(t, rows):
        att_scr[(1 - core) * per_core + t] = rows

    attend(p_refs, v_refs, 1 - core, d // HEADS, put)
    rows = jnp.concatenate(
        [
            jnp.concatenate(
                [att_scr[g, :, i * LANES : (i + 1) * LANES] for g in range(groups)], axis=1
            )
            for i in range(s)
        ],
        axis=0,
    )
    mixed = jnp.dot(rows, wf_ref[...], preferred_element_type=jnp.float32).astype(out_ref.dtype)
    for i in range(s):
        for k in range(n_p):
            start = pl.multiple_of((ids[1] ^ k) * share, share)
            out_ref[i, pl.ds(start, share)] = mixed[i * r + k * share : i * r + (k + 1) * share]


def call(kernel, out_shape, args, ids=None, order=(), hbm=(), scratch=(), flops=0, name=None):
    ins = ((ids,) if ids is not None else ()) + tuple(args) + tuple(hbm) + tuple(order)
    specs = ([SMEM] if ids is not None else []) + [VMEM] * len(args)
    specs += [HBM] * len(hbm) + [ANY] * len(order)
    moved = sum(a.size * a.dtype.itemsize for a in args)
    return pl.pallas_call(
        kernel,
        out_shape=out_shape,
        in_specs=specs,
        out_specs=jax.tree.map(lambda _: VMEM, out_shape),
        scratch_shapes=list(scratch),
        compiler_params=PARAMS,
        cost_estimate=pl.CostEstimate(flops=flops, bytes_accessed=moved, transcendentals=0),
        name=name,
    )(*ins)


def body(n_seq, n_res, x, gain, wq, wk, wv, wf):
    s, r, d = x.shape
    groups = d // LANES
    hsize = d // HEADS
    pack = LANES // hsize
    heads = HEADS // CORES
    blocks = n_seq // CORES
    inner = blocks // 2
    share = r // inner
    cols = r * n_res
    f32, bf16 = jnp.float32, jnp.bfloat16
    shape = jax.ShapeDtypeStruct

    place = lax.axis_index("seq")
    ids = jnp.stack([place & 1, (place >> 1) & (inner - 1)]).astype(jnp.int32)

    def hop(y, k):
        return lax.ppermute(y, "seq", [(i, i ^ k) for i in range(n_seq)])

    part = shape((inner, heads, share, r), f32)
    piece = shape((heads, share, r), f32)
    grouped = shape((groups, r, s * LANES), bf16)
    scratch = [pltpu.VMEM(grouped.shape, bf16)]
    dots = 2 * s * r * d

    def reduce(keep, got, order=()):
        own, *sent = call(
            merge_kernel, (piece,) * inner, (keep, got), ids, order=order, name="merge_scores"
        )
        parts = [hop(y, CORES * (k + 1)) for k, y in enumerate(sent)]
        half = call(sum_kernel, piece, (own, *parts), name="sum_scores")
        return half, hop(half, CORES * inner)

    others = [
        lax.ppermute(x, "res", [(i, (i + k) % n_res) for i in range(n_res)])
        for k in range(1, n_res)
    ]
    q, send, keep = call(
        own_kernel,
        (shape((groups, pack * r, s * LANES), bf16), part, part),
        (gain,),
        ids,
        hbm=(x, wq, wk),
        scratch=[
            pltpu.VMEM(x.shape, bf16),
            pltpu.VMEM(wq.shape, bf16),
            pltpu.VMEM(wk.shape, bf16),
            *scratch,
            pltpu.SemaphoreType.DMA((3,)),
        ],
        flops=dots * (2 * d + r),
        name="own_scores",
    )
    values = [
        call(value_kernel, grouped, (x, gain, wv), order=(send,), flops=dots * d, name="own_values")
    ]
    reduced = [reduce(keep, hop(send, 1), order=values)]
    for other in others:
        send, kept = call(
            send_kernel,
            (part, shape((groups // CORES, r, s * LANES), bf16)),
            (other, gain, wk, q),
            ids,
            order=(reduced[0][0],),
            scratch=scratch,
            flops=dots * (d + r // 2),
            name="other_send",
        )
        keep = call(
            keep_kernel,
            part,
            (kept, q),
            ids,
            order=(send,),
            flops=dots * r // 2,
            name="other_keep",
        )
        value = call(
            value_kernel,
            grouped,
            (other, gain, wv),
            order=(keep,),
            flops=dots * d,
            name="other_values",
        )
        values.append(value)
        reduced.append(reduce(keep, hop(send, 1), order=(value,)))
    scale = float(hsize * s * n_seq) ** -0.5
    probs = call(
        functools.partial(softmax_kernel, scale, n_res),
        shape((heads, share, cols), bf16),
        tuple(a for a, _ in reduced) + tuple(b for _, b in reduced),
        name="softmax",
    )
    mine = [probs] + [hop(probs, CORES * k) for k in range(1, inner)]
    got = [hop(y, 1) for y in mine]
    attended = call(
        functools.partial(attend_kernel, inner, n_res, hsize),
        shape((groups // CORES, r, s * LANES), bf16),
        (*mine, *values),
        ids,
        flops=dots * cols,
        name="attend_mine",
    )
    return call(
        functools.partial(mix_kernel, inner, n_res),
        shape((s, r, d), bf16),
        (*got, *values, attended, wf),
        ids,
        scratch=scratch,
        flops=dots * (d + cols),
        name="mix",
    )


def solution(mesh):
    placed = (P("seq", "res", None), P(), P(), P(), P(), P())
    return jax.shard_map(
        functools.partial(body, mesh.shape["seq"], mesh.shape["res"]),
        mesh=mesh,
        in_specs=placed,
        out_specs=P("seq", "res", None),
        check_vma=False,
    )
```

```python
import functools

import jax
import jax.numpy as jnp
from jax import lax
from jax.experimental import pallas as pl
from jax.experimental.pallas import tpu as pltpu
from jax.sharding import PartitionSpec as P

HEADS = 12
LANES = 128
CORES = 2


VMEM = pl.BlockSpec(memory_space=pltpu.VMEM)
ANY = pl.BlockSpec(memory_space=pl.ANY)
HBM = pl.BlockSpec(memory_space=pltpu.HBM)
PARAMS = pltpu.CompilerParams(vmem_limit_bytes=48 << 20)


def spot(inner):
    place = lax.axis_index("seq")
    return place & (CORES - 1), (place >> 1) & (inner - 1)


def standardize(x, gain):
    x = x.astype(jnp.float32)
    center = x - jnp.mean(x, axis=-1, keepdims=True)
    spread = jnp.mean(center * center, axis=-1, keepdims=True)
    return (center * (1.0 / jnp.sqrt(spread + 1e-05)) * gain).astype(jnp.bfloat16)


def rows_of(x_ref, gain_ref):
    s, r, d = x_ref.shape
    return standardize(x_ref[...].reshape(s * r, d), gain_ref[...].reshape(1, d))


def project(rows, w_ref):
    return jnp.dot(rows, w_ref[...], preferred_element_type=jnp.float32).astype(jnp.bfloat16)


def lane_group(y, s, r, group):
    return jnp.concatenate(
        [y[i * r : (i + 1) * r, group * LANES : (group + 1) * LANES] for i in range(s)], axis=1
    )


def write_scores(q_ref, q_at, k_ref, k_at, out_ref):
    blocks, heads, share, cols = out_ref.shape
    per_core = q_ref.shape[0] // CORES
    pack = heads // per_core
    r = blocks * share
    for t in range(per_core):
        part = lax.dot_general(
            q_ref[q_at + t],
            k_ref[k_at + t],
            (((1,), (1,)), ((), ())),
            preferred_element_type=jnp.float32,
        )
        for h in range(pack):
            out_ref[:, t * pack + h] = part[h * r : (h + 1) * r].reshape(blocks, share, cols)


def own_kernel(
    x_hbm, gain_hbm, wk_hbm, wq_hbm,
    q_ref, send_ref, keep_ref,
    x_ref, gain_ref, wk_ref, wq_ref, k_scr, sems,
):
    pairs = ((x_hbm, x_ref), (gain_hbm, gain_ref), (wk_hbm, wk_ref), (wq_hbm, wq_ref))
    copies = [
        pltpu.make_async_copy(src, dst, sems.at[i]) for i, (src, dst) in enumerate(pairs)
    ]
    for copy in copies:
        copy.start()
    s, r, d = x_ref.shape
    hsize = d // HEADS
    per_core = d // LANES // CORES
    copies[0].wait()
    copies[1].wait()
    rows = rows_of(x_ref, gain_ref)
    copies[2].wait()
    k = project(rows, wk_ref)
    for g in range(d // LANES):
        k_scr[g] = lane_group(k, s, r, g)
    copies[3].wait()
    q = project(rows, wq_ref)
    lane = lax.broadcasted_iota(jnp.int32, (r, s * LANES), 1) % LANES // hsize
    for g in range(d // LANES):
        both = lane_group(q, s, r, g)
        for h in range(LANES // hsize):
            q_ref[g, h * r : (h + 1) * r] = jnp.where(lane == h, both, jnp.zeros_like(both))
    core, _ = spot(1)
    for out_ref, side in ((send_ref, 1 - core), (keep_ref, core)):
        write_scores(q_ref, side * per_core, k_scr, side * per_core, out_ref)


def send_kernel(x_ref, gain_ref, wk_ref, q_ref, after_ref, send_ref, kept_ref, k_scr):
    s, r, d = x_ref.shape
    per_core = d // LANES // CORES
    k = project(rows_of(x_ref, gain_ref), wk_ref)
    for g in range(d // LANES):
        k_scr[g] = lane_group(k, s, r, g)
    core, _ = spot(1)
    write_scores(q_ref, (1 - core) * per_core, k_scr, (1 - core) * per_core, send_ref)
    for t in range(per_core):
        kept_ref[t] = k_scr[core * per_core + t]


def keep_kernel(kept_ref, q_ref, after_ref, keep_ref):
    write_scores(q_ref, spot(1)[0] * kept_ref.shape[0], kept_ref, 0, keep_ref)


def value_kernel(x_ref, gain_ref, wv_ref, after_ref, v_ref):
    s, r, d = x_ref.shape
    v = project(rows_of(x_ref, gain_ref), wv_ref)
    for g in range(d // LANES):
        v_ref[g] = lane_group(v, s, r, g)


def merge_kernel(keep_ref, got_ref, *refs):
    inner = keep_ref.shape[0]
    outs = refs[-inner:]
    _, chip = spot(inner)
    for k, out_ref in enumerate(outs):
        b = chip ^ k
        out_ref[...] = keep_ref[b] + got_ref[b]


def sum_kernel(*refs):
    total = refs[0][...]
    for part in refs[1:-1]:
        total = total + part[...]
    refs[-1][...] = total


def softmax_kernel(scale, n, *refs):
    halves, gots, out_ref = refs[:n], refs[n : 2 * n], refs[2 * n]
    logits = jnp.concatenate([a[...] + b[...] for a, b in zip(halves, gots)], axis=-1) * scale
    p = jnp.exp(logits - jnp.max(logits, axis=-1, keepdims=True))
    out_ref[...] = (p / jnp.sum(p, axis=-1, keepdims=True)).astype(out_ref.dtype)


def attend(p_refs, v_refs, side, hsize, put):
    heads, share, _ = p_refs[0].shape
    pack = LANES // hsize
    r = share * len(p_refs)
    per_core = heads // pack
    width = v_refs[0].shape[-1]
    lane = lax.broadcasted_iota(jnp.int32, (r, width), 1) % LANES // hsize
    for t in range(per_core):
        g = side * per_core + t
        p = jnp.concatenate(
            [p_ref[t * pack + h] for h in range(pack) for p_ref in p_refs], axis=0
        )
        v = jnp.concatenate([v_ref[g] for v_ref in v_refs], axis=0)
        both = jnp.dot(p, v, preferred_element_type=jnp.float32)
        got = both[:r]
        for h in range(1, pack):
            got = jnp.where(lane == h, both[h * r : (h + 1) * r], got)
        put(t, got.astype(jnp.bfloat16))


def attend_kernel(n_p, n_v, hsize, *refs):
    p_refs, v_refs, out_ref = refs[:n_p], refs[n_p : n_p + n_v], refs[-1]

    def put(t, rows):
        out_ref[t] = rows

    attend(p_refs, v_refs, spot(n_p)[0], hsize, put)


def mix_kernel(n_p, n_v, *refs):
    p_refs, v_refs = refs[:n_p], refs[n_p : n_p + n_v]
    mine_ref, wf_ref, out_ref, att_scr = refs[n_p + n_v :]
    s, r, d = out_ref.shape
    share = r // n_p
    groups = d // LANES
    per_core = groups // CORES
    core, chip = spot(n_p)
    for t in range(per_core):
        att_scr[core * per_core + t] = mine_ref[t]

    def put(t, rows):
        att_scr[(1 - core) * per_core + t] = rows

    attend(p_refs, v_refs, 1 - core, d // HEADS, put)
    rows = jnp.concatenate(
        [
            jnp.concatenate(
                [att_scr[g, :, i * LANES : (i + 1) * LANES] for g in range(groups)], axis=1
            )
            for i in range(s)
        ],
        axis=0,
    )
    mixed = jnp.dot(rows, wf_ref[...], preferred_element_type=jnp.float32).astype(out_ref.dtype)
    for i in range(s):
        for k in range(n_p):
            start = pl.multiple_of((chip ^ k) * share, share)
            out_ref[i, pl.ds(start, share)] = mixed[i * r + k * share : i * r + (k + 1) * share]


def call(kernel, out_shape, args, order=(), hbm=(), scratch=(), flops=0, name=None):
    ins = (*args, *(pltpu.with_memory_space_constraint(a, pltpu.HBM) for a in hbm), *order)
    specs = [VMEM] * len(args) + [HBM] * len(hbm) + [ANY] * len(order)
    moved = sum(a.size * a.dtype.itemsize for a in args)
    return pl.pallas_call(
        kernel,
        out_shape=out_shape,
        in_specs=specs,
        out_specs=jax.tree.map(lambda _: VMEM, out_shape),
        scratch_shapes=list(scratch),
        compiler_params=PARAMS,
        cost_estimate=pl.CostEstimate(flops=flops, bytes_accessed=moved, transcendentals=0),
        name=name,
    )(*ins)


def body(n_seq, n_res, x, gain, wq, wk, wv, wf):
    s, r, d = x.shape
    groups = d // LANES
    hsize = d // HEADS
    pack = LANES // hsize
    heads = HEADS // CORES
    blocks = n_seq // CORES
    inner = blocks // 2
    share = r // inner
    cols = r * n_res
    f32, bf16 = jnp.float32, jnp.bfloat16
    shape = jax.ShapeDtypeStruct

    def hop(y, k):
        return lax.ppermute(y, "seq", [(i, i ^ k) for i in range(n_seq)])

    part = shape((inner, heads, share, r), f32)
    piece = shape((heads, share, r), f32)
    grouped = shape((groups, r, s * LANES), bf16)
    scratch = [pltpu.VMEM(grouped.shape, bf16)]
    dots = 2 * s * r * d

    def reduce(keep, got, order=()):
        own, *sent = call(
            merge_kernel, (piece,) * inner, (keep, got), order=order, name="merge_scores"
        )
        parts = [hop(y, CORES * (k + 1)) for k, y in enumerate(sent)]
        half = call(sum_kernel, piece, (own, *parts), name="sum_scores")
        return half, hop(half, CORES * inner)

    others = [
        lax.ppermute(x, "res", [(i, (i + k) % n_res) for i in range(n_res)])
        for k in range(1, n_res)
    ]
    q, send, keep = call(
        own_kernel,
        (shape((groups, pack * r, s * LANES), bf16), part, part),
        (),
        hbm=(x, gain, wk, wq),
        scratch=[
            *(pltpu.VMEM(a.shape, a.dtype) for a in (x, gain, wk, wq)),
            *scratch,
            pltpu.SemaphoreType.DMA((4,)),
        ],
        flops=dots * (2 * d + r),
        name="own_scores",
    )
    values = [
        call(value_kernel, grouped, (x, gain, wv), order=(send,), flops=dots * d, name="own_values")
    ]
    reduced = [reduce(keep, hop(send, 1), order=values)]
    for other in others:
        send, kept = call(
            send_kernel,
            (part, shape((groups // CORES, r, s * LANES), bf16)),
            (other, gain, wk, q),
            order=(reduced[0][0],),
            scratch=scratch,
            flops=dots * (d + r // 2),
            name="other_send",
        )
        keep = call(
            keep_kernel,
            part,
            (kept, q),
            order=(send,),
            flops=dots * r // 2,
            name="other_keep",
        )
        value = call(
            value_kernel,
            grouped,
            (other, gain, wv),
            order=(keep,),
            flops=dots * d,
            name="other_values",
        )
        values.append(value)
        reduced.append(reduce(keep, hop(send, 1), order=(value,)))
    scale = float(hsize * s * n_seq) ** -0.5
    probs = call(
        functools.partial(softmax_kernel, scale, n_res),
        shape((heads, share, cols), bf16),
        tuple(a for a, _ in reduced) + tuple(b for _, b in reduced),
        name="softmax",
    )
    mine = [probs] + [hop(probs, CORES * k) for k in range(1, inner)]
    got = [hop(y, 1) for y in mine]
    attended = call(
        functools.partial(attend_kernel, inner, n_res, hsize),
        shape((groups // CORES, r, s * LANES), bf16),
        (*mine, *values),
        flops=dots * cols,
        name="attend_mine",
    )
    return call(
        functools.partial(mix_kernel, inner, n_res),
        shape((s, r, d), bf16),
        (*got, *values, attended, wf),
        scratch=scratch,
        flops=dots * (d + cols),
        name="mix",
    )


def solution(mesh):
    placed = (P("seq", "res", None), P(), P(), P(), P(), P())
    return jax.shard_map(
        functools.partial(body, mesh.shape["seq"], mesh.shape["res"]),
        mesh=mesh,
        in_specs=placed,
        out_specs=P("seq", "res", None),
        check_vma=False,
    )
```

```python
import functools

import jax
import jax.numpy as jnp
from jax import lax
from jax.experimental import pallas as pl
from jax.experimental.pallas import tpu as pltpu
from jax.sharding import PartitionSpec as P

HEADS = 12
LANES = 128
CORES = 2


VMEM = pl.BlockSpec(memory_space=pltpu.VMEM)
ANY = pl.BlockSpec(memory_space=pl.ANY)
HBM = pl.BlockSpec(memory_space=pltpu.HBM)
PARAMS = pltpu.CompilerParams(vmem_limit_bytes=48 << 20)


def spot(inner):
    place = lax.axis_index("seq")
    return place & (CORES - 1), (place >> 1) & (inner - 1)


def standardize(x, gain):
    x = x.astype(jnp.float32)
    center = x - jnp.mean(x, axis=-1, keepdims=True)
    spread = jnp.mean(center * center, axis=-1, keepdims=True)
    return (center * (1.0 / jnp.sqrt(spread + 1e-05)) * gain).astype(jnp.bfloat16)


def rows_of(x_ref, gain_ref):
    s, r, d = x_ref.shape
    return standardize(x_ref[...].reshape(s * r, d), gain_ref[...].reshape(1, d))


def project(rows, w_ref):
    return jnp.dot(rows, w_ref[...], preferred_element_type=jnp.float32).astype(jnp.bfloat16)


def lane_group(y, s, r, group):
    return jnp.concatenate(
        [y[i * r : (i + 1) * r, group * LANES : (group + 1) * LANES] for i in range(s)], axis=1
    )


def half_of(w_ref, side):
    half = w_ref.shape[1] // CORES
    return w_ref.at[:, pl.ds(pl.multiple_of(side * half, half), half)]


def write_keys(rows, w_ref, s, k_scr):
    k = project(rows, w_ref)
    for g in range(k_scr.shape[0]):
        k_scr[g] = lane_group(k, s, k_scr.shape[1], g)


def write_queries(rows, w_ref, s, hsize, q_ref):
    q = project(rows, w_ref)
    pack = LANES // hsize
    r = q_ref.shape[1] // pack
    lane = lax.broadcasted_iota(jnp.int32, (r, s * LANES), 1) % LANES // hsize
    for g in range(q_ref.shape[0]):
        both = lane_group(q, s, r, g)
        for h in range(pack):
            q_ref[g, h * r : (h + 1) * r] = jnp.where(lane == h, both, jnp.zeros_like(both))


def write_scores(q_ref, k_ref, out_ref):
    blocks, heads, share, cols = out_ref.shape
    pack = heads // q_ref.shape[0]
    r = blocks * share
    for t in range(q_ref.shape[0]):
        part = lax.dot_general(
            q_ref[t], k_ref[t], (((1,), (1,)), ((), ())), preferred_element_type=jnp.float32
        )
        for h in range(pack):
            out_ref[:, t * pack + h] = part[h * r : (h + 1) * r].reshape(blocks, share, cols)


def load(pairs, sems):
    copies = [pltpu.make_async_copy(a, b, sems.at[i]) for i, (a, b) in enumerate(pairs)]
    for copy in copies:
        copy.start()
    return copies


def own_send_kernel(
    x_hbm, gain_hbm, wk_hbm, wq_hbm,
    rows_ref, q_ref, send_ref,
    x_ref, gain_ref, wk_ref, wq_ref, k_scr, sems,
):
    side = 1 - spot(1)[0]
    copies = load(
        (
            (x_hbm, x_ref),
            (gain_hbm, gain_ref),
            (half_of(wk_hbm, side), wk_ref),
            (half_of(wq_hbm, side), wq_ref),
        ),
        sems,
    )
    s, _, d = x_ref.shape
    copies[0].wait()
    copies[1].wait()
    rows_ref[...] = rows_of(x_ref, gain_ref)
    copies[2].wait()
    write_keys(rows_ref[...], wk_ref, s, k_scr)
    copies[3].wait()
    write_queries(rows_ref[...], wq_ref, s, d // HEADS, q_ref)
    write_scores(q_ref, k_scr, send_ref)


def own_keep_kernel(
    rows_ref, wk_hbm, wq_hbm, after_ref, q_ref, keep_ref, wk_ref, wq_ref, k_scr, sems
):
    side = spot(1)[0]
    copies = load(((half_of(wk_hbm, side), wk_ref), (half_of(wq_hbm, side), wq_ref)), sems)
    d = rows_ref.shape[1]
    s = rows_ref.shape[0] // k_scr.shape[1]
    copies[0].wait()
    write_keys(rows_ref[...], wk_ref, s, k_scr)
    copies[1].wait()
    write_queries(rows_ref[...], wq_ref, s, d // HEADS, q_ref)
    write_scores(q_ref, k_scr, keep_ref)


def send_kernel(x_ref, gain_ref, wk_ref, q_ref, after_ref, rows_ref, send_ref, k_scr):
    rows_ref[...] = rows_of(x_ref, gain_ref)
    write_keys(rows_ref[...], half_of(wk_ref, 1 - spot(1)[0]), x_ref.shape[0], k_scr)
    write_scores(q_ref, k_scr, send_ref)


def keep_kernel(rows_ref, wk_ref, q_ref, after_ref, keep_ref, k_scr):
    s = rows_ref.shape[0] // k_scr.shape[1]
    write_keys(rows_ref[...], half_of(wk_ref, spot(1)[0]), s, k_scr)
    write_scores(q_ref, k_scr, keep_ref)


def value_kernel(rows_ref, wv_hbm, after_ref, v_ref, wv_ref, sems):
    groups, r, width = v_ref.shape
    for copy in load(((wv_hbm, wv_ref),), sems):
        copy.wait()
    v = project(rows_ref[...], wv_ref)
    for g in range(groups):
        v_ref[g] = lane_group(v, width // LANES, r, g)


def steps(inner):
    return sorted(range(inner), key=lambda k: (k > 0, -k.bit_count(), k))


def merge_kernel(keep_ref, got_ref, *refs):
    inner = keep_ref.shape[0]
    outs = refs[-inner:]
    _, chip = spot(inner)
    for k, out_ref in zip(steps(inner), outs):
        b = chip ^ k
        out_ref[...] = keep_ref[b] + got_ref[b]


def sum_kernel(n, *refs):
    total = refs[0][...]
    for part in refs[1:n]:
        total = total + part[...]
    refs[-1][...] = total


def own_softmax_kernel(scale, mine_ref, other_ref, after_ref, p_ref, top_ref, sum_ref):
    logits = (mine_ref[...] + other_ref[...]) * scale
    top = jnp.max(logits, axis=-1, keepdims=True)
    p = jnp.exp(logits - top)
    p_ref[...] = p.astype(p_ref.dtype)
    top_ref[...] = jnp.broadcast_to(top, top_ref.shape)
    sum_ref[...] = jnp.broadcast_to(jnp.sum(p, axis=-1, keepdims=True), sum_ref.shape)


def softmax_kernel(scale, n, *refs):
    mine, other, (own_top_ref, own_sum_ref, out_ref) = refs[:n], refs[n : 2 * n], refs[2 * n :]
    logits = jnp.concatenate([a[...] + b[...] for a, b in zip(mine, other)], axis=-1) * scale
    heads, share, cols = logits.shape
    own_top = own_top_ref[...][..., :1]
    top = jnp.maximum(own_top, jnp.max(logits, axis=-1, keepdims=True))
    p = jnp.exp(logits - top)
    factor = jnp.exp(own_top - top)
    total = own_sum_ref[...][..., :1] * factor + jnp.sum(p, axis=-1, keepdims=True)
    out_ref[:heads] = (p / total).astype(out_ref.dtype)
    factor = factor / total
    high = factor.astype(out_ref.dtype).astype(jnp.float32)
    low = factor - high
    lane = lax.broadcasted_iota(jnp.int32, (share, cols), 1)
    packed = jnp.zeros((share, cols), jnp.float32)
    for h in range(heads):
        packed = jnp.where(lane == h, high[h], packed)
        packed = jnp.where(lane == heads + h, low[h], packed)
    out_ref[heads] = packed.astype(out_ref.dtype)


def pack_kernel(n, *refs):
    for k in range(n):
        refs[-1][k] = refs[k][...]


def weighted(p_ref, v_refs, g, t, hsize):
    pieces, _, share, _ = p_ref.shape
    pack = LANES // hsize
    r = pieces * share
    p = jnp.concatenate(
        [p_ref[:, t * pack + h].reshape(r, p_ref.shape[-1]) for h in range(pack)], axis=0
    )
    v = jnp.concatenate([v_ref[g] for v_ref in v_refs], axis=0)
    both = jnp.dot(p, v, preferred_element_type=jnp.float32)
    return pick([both[h * r : (h + 1) * r] for h in range(pack)], both.shape[1], hsize)


def pick(per_head, width, hsize):
    r = per_head[0].shape[0]
    lane = lax.broadcasted_iota(jnp.int32, (r, width), 1) % LANES // hsize
    got = jnp.broadcast_to(per_head[0], (r, width))
    for h in range(1, len(per_head)):
        got = jnp.where(lane == h, per_head[h], got)
    return got


def own_attend_kernel(hsize, mine_ref, got_ref, v_ref, out_ref):
    core = spot(mine_ref.shape[0])[0]
    per_core = v_ref.shape[0] // CORES
    for p_ref, side in ((mine_ref, core), (got_ref, 1 - core)):
        for t in range(per_core):
            g = side * per_core + t
            out_ref[g] = weighted(p_ref, (v_ref,), g, t, hsize)


def attended(p_ref, v_refs, own_ref, side, hsize):
    pieces, heads, share, _ = p_ref.shape
    heads -= 1
    pack = LANES // hsize
    per_core = heads // pack
    width = own_ref.shape[-1]
    groups = []
    for t in range(per_core):
        g = side * per_core + t
        factors = []
        for h in range(t * pack, (t + 1) * pack):
            packed = p_ref[:, heads].reshape(pieces * share, -1).astype(jnp.float32)
            factors.append(packed[:, h : h + 1] + packed[:, heads + h : heads + h + 1])
        own = own_ref[g] * pick(factors, width, hsize)
        groups.append((own + weighted(p_ref, v_refs, g, t, hsize)).astype(jnp.bfloat16))
    return jnp.concatenate(
        [
            jnp.concatenate([g[:, i : i + LANES] for g in groups], axis=1)
            for i in range(0, width, LANES)
        ],
        axis=0,
    )


def half_rows(w_ref, side):
    half = w_ref.shape[0] // CORES
    return w_ref[pl.ds(pl.multiple_of(side * half, half), half)]


def half_mix_kernel(hsize, n, p_ref, *refs):
    v_refs, (own_ref, wf_ref, out_ref) = refs[:n], refs[n:]
    side = spot(p_ref.shape[0])[0]
    rows = attended(p_ref, v_refs, own_ref, side, hsize)
    out_ref[...] = jnp.dot(rows, half_rows(wf_ref, side), preferred_element_type=jnp.float32)


def mix_kernel(hsize, n, p_ref, *refs):
    v_refs, (own_ref, half_ref, wf_ref, out_hbm, out_ref, sems) = refs[:n], refs[n:]
    pieces = p_ref.shape[0]
    s, r, _ = out_ref.shape
    share = r // pieces
    core, chip = spot(pieces)
    rows = attended(p_ref, v_refs, own_ref, 1 - core, hsize)
    w = half_rows(wf_ref, 1 - core)
    copies = []
    for i in range(s):
        part = slice(i * r, (i + 1) * r)
        mixed = half_ref[part] + jnp.dot(rows[part], w, preferred_element_type=jnp.float32)
        mixed = mixed.astype(out_ref.dtype)
        for n, k in enumerate(steps(pieces)):
            start = pl.multiple_of((chip ^ k) * share, share)
            out_ref[i, pl.ds(start, share)] = mixed[n * share : (n + 1) * share]
        copies.append(pltpu.make_async_copy(out_ref.at[i], out_hbm.at[i], sems.at[i]))
        copies[-1].start()
    for copy in copies:
        copy.wait()


def call(kernel, out_shape, args, order=(), hbm=(), scratch=(), flops=0, out_space=VMEM):
    ins = (*args, *(pltpu.with_memory_space_constraint(a, pltpu.HBM) for a in hbm), *order)
    specs = [VMEM] * len(args) + [HBM] * len(hbm) + [ANY] * len(order)
    moved = sum(a.size * a.dtype.itemsize for a in args)
    return pl.pallas_call(
        kernel,
        out_shape=out_shape,
        in_specs=specs,
        out_specs=jax.tree.map(lambda _: out_space, out_shape),
        scratch_shapes=list(scratch),
        compiler_params=PARAMS,
        cost_estimate=pl.CostEstimate(flops=flops, bytes_accessed=moved, transcendentals=0),
    )(*ins)


def body(n_seq, n_res, x, gain, wq, wk, wv, wf):
    s, r, d = x.shape
    groups = d // LANES
    hsize = d // HEADS
    pack = LANES // hsize
    heads = HEADS // CORES
    blocks = n_seq // CORES
    inner = blocks // 2
    share = r // inner
    cols = r * n_res
    f32, bf16 = jnp.float32, jnp.bfloat16
    shape = jax.ShapeDtypeStruct

    part = shape((inner, heads, share, r), f32)
    piece = shape((heads, share, r), f32)
    normed = shape((s * r, d), bf16)
    grouped = shape((groups, r, s * LANES), bf16)
    queries = shape((groups // CORES, pack * r, s * LANES), bf16)
    keys = pltpu.VMEM((groups // CORES, r, s * LANES), bf16)
    half = pltpu.VMEM((d, d // CORES), bf16)
    dots = 2 * s * r * d

    def hop(y, k):
        return lax.ppermute(y, "seq", [(i, i ^ k) for i in range(n_seq)])

    def values_of(rows, order):
        return call(
            value_kernel,
            grouped,
            (rows,),
            hbm=(wv,),
            order=order,
            scratch=[pltpu.VMEM(wv.shape, bf16), pltpu.SemaphoreType.DMA((1,))],
            flops=dots * d,
        )

    def split(keep, got, order=()):
        return call(merge_kernel, (piece,) * inner, (keep, got), order=order)

    def reduce(own, *sent, order=()):
        parts = [hop(y, CORES * k) for k, y in zip(steps(inner)[1:], sent)]
        total = call(functools.partial(sum_kernel, inner), piece, (own, *parts), order=order)
        return total, hop(total, CORES * inner)

    others = [
        lax.ppermute(x, "res", [(i, (i + k) % n_res) for i in range(n_res)])
        for k in range(1, n_res)
    ]
    rows, q_send, send = call(
        own_send_kernel,
        (normed, queries, part),
        (),
        hbm=(x, gain, wk, wq),
        scratch=[
            pltpu.VMEM(x.shape, bf16),
            pltpu.VMEM(gain.shape, f32),
            half,
            half,
            keys,
            pltpu.SemaphoreType.DMA((4,)),
        ],
        flops=dots * (d + r // 2),
    )
    got = hop(send, 1)
    q_keep, keep = call(
        own_keep_kernel,
        (queries, part),
        (rows,),
        hbm=(wk, wq),
        order=(send,),
        scratch=[half, half, keys, pltpu.SemaphoreType.DMA((2,))],
        flops=dots * (d + r // 2),
    )
    pieces = split(keep, got)
    values = [values_of(rows, pieces[:1])]
    reduced = [reduce(*pieces, order=values)]
    for other in others:
        rows, send = call(
            send_kernel,
            (normed, part),
            (other, gain, wk, q_send),
            order=(reduced[0][0],),
            scratch=[keys],
            flops=dots * (d // 2 + r // 2),
        )
        got = hop(send, 1)
        keep = call(
            keep_kernel,
            part,
            (rows, wk, q_keep),
            order=(send,),
            scratch=[keys],
            flops=dots * (d // 2 + r // 2),
        )
        pieces = split(keep, got)
        values.append(values_of(rows, pieces[:1]))
        reduced.append(reduce(*pieces, order=values[-1:]))
    scale = float(hsize * s * n_seq) ** -0.5

    def gather(y, order=()):
        mine = [y] + [hop(y, CORES * k) for k in steps(inner)[1:]]
        mine = call(
            functools.partial(pack_kernel, inner), shape((inner, *y.shape), bf16), mine, order=order
        )
        return mine, hop(mine, 1)

    own_probs, own_top, own_sum = call(
        functools.partial(own_softmax_kernel, scale),
        (shape(piece.shape, bf16), piece, piece),
        reduced[0],
        order=(reduced[-1][0],),
    )
    probs = call(
        functools.partial(softmax_kernel, scale, n_res - 1),
        shape((heads + 1, share, cols - r), bf16),
        (*(a for a, _ in reduced[1:]), *(b for _, b in reduced[1:]), own_top, own_sum),
    )
    own_mine, own_got = gather(own_probs, order=(probs,))
    own_part = call(
        functools.partial(own_attend_kernel, hsize),
        shape(grouped.shape, f32),
        (own_mine, own_got, values[0]),
        flops=dots * r,
    )
    mine, got = gather(probs, order=(own_part,))
    half_mix = call(
        functools.partial(half_mix_kernel, hsize, n_res - 1),
        shape((s * r, d), f32),
        (mine, *values[1:], own_part, wf),
        flops=dots * (d + cols) // 2,
    )
    return call(
        functools.partial(mix_kernel, hsize, n_res - 1),
        shape((s, r, d), bf16),
        (got, *values[1:], own_part, half_mix, wf),
        scratch=[pltpu.VMEM(x.shape, bf16), pltpu.SemaphoreType.DMA((s,))],
        flops=dots * (d + cols) // 2,
        out_space=HBM,
    )


def solution(mesh):
    n_seq, n_res = mesh.shape["seq"], mesh.shape["res"]

    def program(*args):
        return body(n_seq, n_res, *args)

    placed = (P("seq", "res", None), P(), P(), P(), P(), P())
    return jax.shard_map(
        program, mesh=mesh, in_specs=placed, out_specs=P("seq", "res", None), check_vma=False
    )
```

```python
import functools

import jax
import jax.numpy as jnp
from jax import lax
from jax.experimental import pallas as pl
from jax.experimental.pallas import tpu as pltpu
from jax.sharding import PartitionSpec as P

HEADS = 12
LANES = 128
CORES = 2

UNIT = 0.5
CODED = 80.0


VMEM = pl.BlockSpec(memory_space=pltpu.VMEM)
ANY = pl.BlockSpec(memory_space=pl.ANY)
HBM = pl.BlockSpec(memory_space=pltpu.HBM)
PARAMS = pltpu.CompilerParams(vmem_limit_bytes=48 << 20)


def spot(inner):
    place = lax.axis_index("seq")
    return place & (CORES - 1), (place >> 1) & (inner - 1)


def standardize(x, gain):
    x = x.astype(jnp.float32)
    center = x - jnp.mean(x, axis=-1, keepdims=True)
    spread = jnp.mean(center * center, axis=-1, keepdims=True)
    return (center * (1.0 / jnp.sqrt(spread + 1e-05)) * gain).astype(jnp.bfloat16)


def rows_of(x_ref, gain_ref):
    s, r, d = x_ref.shape
    return standardize(x_ref[...].reshape(s * r, d), gain_ref[...].reshape(1, d))


def project(rows, w_ref):
    return jnp.dot(rows, w_ref[...], preferred_element_type=jnp.float32).astype(jnp.bfloat16)


def lane_group(y, s, r, group):
    return jnp.concatenate(
        [y[i * r : (i + 1) * r, group * LANES : (group + 1) * LANES] for i in range(s)], axis=1
    )


def half_of(w_ref, side):
    half = w_ref.shape[1] // CORES
    return w_ref.at[:, pl.ds(pl.multiple_of(side * half, half), half)]


def write_keys(rows, w_ref, s, k_scr):
    k = project(rows, w_ref)
    for g in range(k_scr.shape[0]):
        k_scr[g] = lane_group(k, s, k_scr.shape[1], g)


def write_queries(rows, w_ref, s, hsize, q_ref):
    q = project(rows, w_ref)
    pack = LANES // hsize
    r = q_ref.shape[1] // pack
    lane = lax.broadcasted_iota(jnp.int32, (r, s * LANES), 1) % LANES // hsize
    for g in range(q_ref.shape[0]):
        both = lane_group(q, s, r, g)
        for h in range(pack):
            q_ref[g, h * r : (h + 1) * r] = jnp.where(lane == h, both, jnp.zeros_like(both))


def write_scores(q_ref, k_ref, out_ref):
    blocks, heads, share, cols = out_ref.shape
    pack = heads // q_ref.shape[0]
    r = blocks * share
    for t in range(q_ref.shape[0]):
        part = lax.dot_general(
            q_ref[t], k_ref[t], (((1,), (1,)), ((), ())), preferred_element_type=jnp.float32
        )
        for h in range(pack):
            out_ref[:, t * pack + h] = part[h * r : (h + 1) * r].reshape(blocks, share, cols)


def load(pairs, sems):
    copies = [pltpu.make_async_copy(a, b, sems.at[i]) for i, (a, b) in enumerate(pairs)]
    for copy in copies:
        copy.start()
    return copies


def own_send_kernel(
    x_hbm, gain_hbm, wk_hbm, wq_hbm,
    rows_ref, q_ref, send_ref,
    x_ref, gain_ref, wk_ref, wq_ref, k_scr, sems,
):
    side = 1 - spot(1)[0]
    copies = load(
        (
            (x_hbm, x_ref),
            (gain_hbm, gain_ref),
            (half_of(wk_hbm, side), wk_ref),
            (half_of(wq_hbm, side), wq_ref),
        ),
        sems,
    )
    s, _, d = x_ref.shape
    copies[0].wait()
    copies[1].wait()
    rows_ref[...] = rows_of(x_ref, gain_ref)
    copies[2].wait()
    write_keys(rows_ref[...], wk_ref, s, k_scr)
    copies[3].wait()
    write_queries(rows_ref[...], wq_ref, s, d // HEADS, q_ref)
    write_scores(q_ref, k_scr, send_ref)


def own_keep_kernel(
    rows_ref, wk_hbm, wq_hbm, after_ref, q_ref, keep_ref, wk_ref, wq_ref, k_scr, sems
):
    side = spot(1)[0]
    copies = load(((half_of(wk_hbm, side), wk_ref), (half_of(wq_hbm, side), wq_ref)), sems)
    d = rows_ref.shape[1]
    s = rows_ref.shape[0] // k_scr.shape[1]
    copies[0].wait()
    write_keys(rows_ref[...], wk_ref, s, k_scr)
    copies[1].wait()
    write_queries(rows_ref[...], wq_ref, s, d // HEADS, q_ref)
    write_scores(q_ref, k_scr, keep_ref)


def send_kernel(x_ref, gain_ref, wk_ref, q_ref, after_ref, rows_ref, send_ref, k_scr):
    rows_ref[...] = rows_of(x_ref, gain_ref)
    write_keys(rows_ref[...], half_of(wk_ref, 1 - spot(1)[0]), x_ref.shape[0], k_scr)
    write_scores(q_ref, k_scr, send_ref)


def keep_kernel(rows_ref, wk_ref, q_ref, after_ref, keep_ref, k_scr):
    s = rows_ref.shape[0] // k_scr.shape[1]
    write_keys(rows_ref[...], half_of(wk_ref, spot(1)[0]), s, k_scr)
    write_scores(q_ref, k_scr, keep_ref)


def write_values(rows, wv, v_ref):
    groups, r, width = v_ref.shape
    v = project(rows, wv)
    for g in range(groups):
        v_ref[g] = lane_group(v, width // LANES, r, g)


def own_value_kernel(rows_ref, wv_hbm, wf_hbm, after_ref, v_ref, wv_ref, wf_ref, sems):
    copies = load(((wv_hbm, wv_ref), (wf_hbm, wf_ref)), sems)
    copies[0].wait()
    write_values(rows_ref[...], wv_ref, v_ref)
    copies[1].wait()


def value_kernel(rows_ref, wv_ref, after_ref, v_ref):
    write_values(rows_ref[...], wv_ref, v_ref)


def encode(u):
    near = jnp.exp(jnp.clip(u, -CODED, CODED))
    far = jnp.where(u < 0, u, -1.0 / u)
    return jnp.where(jnp.abs(u) < CODED, near, far).astype(jnp.bfloat16)


def decode(y):
    y = y.astype(jnp.float32)
    near = jnp.log(jnp.abs(y))
    far = jnp.where(y < -1.0, y, -1.0 / y)
    return jnp.where(y > 0, near, far)


def steps(inner):
    return sorted(range(inner), key=lambda k: (k > 0, -k.bit_count(), k))


def merge_kernel(factor, keep_ref, got_ref, *refs):
    inner = keep_ref.shape[0]
    if refs[-1].shape == keep_ref.shape:
        outs, top_out, top_ref = refs[:-1], refs[-1], None
    else:
        outs, top_out, top_ref = refs[1:], None, refs[0]
    _, chip = spot(inner)
    for k, out_ref in zip(steps(inner), outs):
        b = chip ^ k
        u = (keep_ref[b] + got_ref[b]) * factor
        if top_out is None:
            top = top_ref[b]
        else:
            top = jnp.broadcast_to(jnp.max(u, axis=-1, keepdims=True), u.shape)
            top_out[b] = top
        u = u - top
        out_ref[...] = encode(u) if k else u


def sum_kernel(n, own_ref, *refs):
    total = own_ref[...]
    for part in refs[: n - 1]:
        total = total + decode(part[...])
    refs[-2][...] = total
    refs[-1][...] = encode(total * 0.5)


def logits_of(mine_ref, other_ref):
    return (mine_ref[...] + 2.0 * decode(other_ref[...])) * UNIT


def own_softmax_kernel(mine_ref, other_ref, after_ref, p_ref, top_ref, sum_ref):
    logits = logits_of(mine_ref, other_ref)
    top = jnp.max(logits, axis=-1, keepdims=True)
    p = jnp.exp(logits - top)
    p_ref[...] = p.astype(p_ref.dtype)
    top_ref[...] = jnp.broadcast_to(top, top_ref.shape)
    sum_ref[...] = jnp.broadcast_to(jnp.sum(p, axis=-1, keepdims=True), sum_ref.shape)


def softmax_kernel(n, *refs):
    mine, other, (own_top_ref, own_sum_ref, out_ref) = refs[:n], refs[n : 2 * n], refs[2 * n :]
    logits = jnp.concatenate([logits_of(a, b) for a, b in zip(mine, other)], axis=-1)
    heads, share, cols = logits.shape
    own_top = own_top_ref[...][..., :1]
    top = jnp.maximum(own_top, jnp.max(logits, axis=-1, keepdims=True))
    p = jnp.exp(logits - top)
    factor = jnp.exp(own_top - top)
    total = own_sum_ref[...][..., :1] * factor + jnp.sum(p, axis=-1, keepdims=True)
    out_ref[:heads] = (p / total).astype(out_ref.dtype)
    factor = factor / total
    high = factor.astype(out_ref.dtype).astype(jnp.float32)
    low = factor - high
    lane = lax.broadcasted_iota(jnp.int32, (share, cols), 1)
    packed = jnp.zeros((share, cols), jnp.float32)
    for h in range(heads):
        packed = jnp.where(lane == h, high[h], packed)
        packed = jnp.where(lane == heads + h, low[h], packed)
    out_ref[heads] = packed.astype(out_ref.dtype)


def pack_kernel(n, *refs):
    for k in range(n):
        refs[-1][k] = refs[k][...]


def weighted(p_ref, v_refs, g, t, hsize):
    pieces, _, share, _ = p_ref.shape
    pack = LANES // hsize
    r = pieces * share
    p = jnp.concatenate(
        [p_ref[:, t * pack + h].reshape(r, p_ref.shape[-1]) for h in range(pack)], axis=0
    )
    v = jnp.concatenate([v_ref[g] for v_ref in v_refs], axis=0)
    both = jnp.dot(p, v, preferred_element_type=jnp.float32)
    return pick([both[h * r : (h + 1) * r] for h in range(pack)], both.shape[1], hsize)


def pick(per_head, width, hsize):
    r = per_head[0].shape[0]
    lane = lax.broadcasted_iota(jnp.int32, (r, width), 1) % LANES // hsize
    got = jnp.broadcast_to(per_head[0], (r, width))
    for h in range(1, len(per_head)):
        got = jnp.where(lane == h, per_head[h], got)
    return got


def own_attend_kernel(hsize, mine_ref, got_ref, v_ref, out_ref):
    core = spot(mine_ref.shape[0])[0]
    per_core = v_ref.shape[0] // CORES
    for p_ref, side in ((mine_ref, core), (got_ref, 1 - core)):
        for t in range(per_core):
            g = side * per_core + t
            out_ref[g] = weighted(p_ref, (v_ref,), g, t, hsize)


def attended(p_ref, v_refs, own_ref, side, hsize):
    pieces, heads, share, _ = p_ref.shape
    heads -= 1
    pack = LANES // hsize
    per_core = heads // pack
    width = own_ref.shape[-1]
    groups = []
    for t in range(per_core):
        g = side * per_core + t
        factors = []
        for h in range(t * pack, (t + 1) * pack):
            packed = p_ref[:, heads].reshape(pieces * share, -1).astype(jnp.float32)
            factors.append(packed[:, h : h + 1] + packed[:, heads + h : heads + h + 1])
        own = own_ref[g] * pick(factors, width, hsize)
        groups.append((own + weighted(p_ref, v_refs, g, t, hsize)).astype(jnp.bfloat16))
    return jnp.concatenate(
        [
            jnp.concatenate([g[:, i : i + LANES] for g in groups], axis=1)
            for i in range(0, width, LANES)
        ],
        axis=0,
    )


def half_rows(w_ref, side):
    half = w_ref.shape[0] // CORES
    return w_ref[pl.ds(pl.multiple_of(side * half, half), half)]


def half_mix_kernel(hsize, n, p_ref, *refs):
    v_refs, (own_ref, wf_ref, out_ref) = refs[:n], refs[n:]
    side = spot(p_ref.shape[0])[0]
    rows = attended(p_ref, v_refs, own_ref, side, hsize)
    out_ref[...] = jnp.dot(rows, half_rows(wf_ref, side), preferred_element_type=jnp.float32)


def mix_kernel(hsize, n, p_ref, *refs):
    v_refs, (own_ref, half_ref, wf_ref, out_hbm, out_ref, sems) = refs[:n], refs[n:]
    pieces = p_ref.shape[0]
    s, r, _ = out_ref.shape
    share = r // pieces
    core, chip = spot(pieces)
    rows = attended(p_ref, v_refs, own_ref, 1 - core, hsize)
    w = half_rows(wf_ref, 1 - core)
    copies = []
    for i in range(s):
        part = slice(i * r, (i + 1) * r)
        mixed = half_ref[part] + jnp.dot(rows[part], w, preferred_element_type=jnp.float32)
        mixed = mixed.astype(out_ref.dtype)
        for n, k in enumerate(steps(pieces)):
            start = pl.multiple_of((chip ^ k) * share, share)
            out_ref[i, pl.ds(start, share)] = mixed[n * share : (n + 1) * share]
        copies.append(pltpu.make_async_copy(out_ref.at[i], out_hbm.at[i], sems.at[i]))
        copies[-1].start()
    for copy in copies:
        copy.wait()


def call(kernel, out_shape, args, order=(), hbm=(), scratch=(), flops=0, out_space=VMEM):
    ins = (*args, *(pltpu.with_memory_space_constraint(a, pltpu.HBM) for a in hbm), *order)
    specs = [VMEM] * len(args) + [HBM] * len(hbm) + [ANY] * len(order)
    moved = sum(a.size * a.dtype.itemsize for a in args)
    return pl.pallas_call(
        kernel,
        out_shape=out_shape,
        in_specs=specs,
        out_specs=jax.tree.map(lambda _: out_space, out_shape),
        scratch_shapes=list(scratch),
        compiler_params=PARAMS,
        cost_estimate=pl.CostEstimate(flops=flops, bytes_accessed=moved, transcendentals=0),
    )(*ins)


def body(n_seq, n_res, x, gain, wq, wk, wv, wf):
    s, r, d = x.shape
    groups = d // LANES
    hsize = d // HEADS
    pack = LANES // hsize
    heads = HEADS // CORES
    blocks = n_seq // CORES
    inner = blocks // 2
    share = r // inner
    cols = r * n_res
    f32, bf16 = jnp.float32, jnp.bfloat16
    shape = jax.ShapeDtypeStruct

    part = shape((inner, heads, share, r), f32)
    piece = shape((heads, share, r), f32)
    normed = shape((s * r, d), bf16)
    grouped = shape((groups, r, s * LANES), bf16)
    queries = shape((groups // CORES, pack * r, s * LANES), bf16)
    keys = pltpu.VMEM((groups // CORES, r, s * LANES), bf16)
    half = pltpu.VMEM((d, d // CORES), bf16)
    dots = 2 * s * r * d

    def hop(y, k):
        return lax.ppermute(y, "seq", [(i, i ^ k) for i in range(n_seq)])

    coded = shape((heads, share, r), bf16)
    scale = float(hsize * s * n_seq) ** -0.5
    merge = functools.partial(merge_kernel, scale / UNIT)

    def reduce(own, *sent, order=()):
        parts = [hop(y, CORES * k) for k, y in zip(steps(inner)[1:], sent)]
        total, half = call(
            functools.partial(sum_kernel, inner), (piece, coded), (own, *parts), order=order
        )
        return total, hop(half, CORES * inner)

    others = [
        lax.ppermute(x, "res", [(i, (i + k) % n_res) for i in range(n_res)])
        for k in range(1, n_res)
    ]
    rows, q_send, send = call(
        own_send_kernel,
        (normed, queries, part),
        (),
        hbm=(x, gain, wk, wq),
        scratch=[
            pltpu.VMEM(x.shape, bf16),
            pltpu.VMEM(gain.shape, f32),
            half,
            half,
            keys,
            pltpu.SemaphoreType.DMA((4,)),
        ],
        flops=dots * (d + r // 2),
    )
    got = hop(send, 1)
    q_keep, keep = call(
        own_keep_kernel,
        (queries, part),
        (rows,),
        hbm=(wk, wq),
        order=(send,),
        scratch=[half, half, keys, pltpu.SemaphoreType.DMA((2,))],
        flops=dots * (d + r // 2),
    )
    *pieces, top = call(merge, (piece, *[coded] * (inner - 1), part), (keep, got))
    value, wv, wf = call(
        own_value_kernel,
        (grouped, shape(wv.shape, bf16), shape(wf.shape, bf16)),
        (rows,),
        hbm=(wv, wf),
        order=pieces[:1],
        scratch=[pltpu.SemaphoreType.DMA((2,))],
        flops=dots * d,
    )
    values = [value]
    reduced = [reduce(*pieces, order=values)]
    for other in others:
        rows, send = call(
            send_kernel,
            (normed, part),
            (other, gain, wk, q_send),
            order=(reduced[0][0],),
            scratch=[keys],
            flops=dots * (d // 2 + r // 2),
        )
        got = hop(send, 1)
        keep = call(
            keep_kernel,
            part,
            (rows, wk, q_keep),
            order=(send,),
            scratch=[keys],
            flops=dots * (d // 2 + r // 2),
        )
        pieces = call(merge, (piece, *[coded] * (inner - 1)), (keep, got, top))
        values.append(call(value_kernel, grouped, (rows, wv), order=pieces[:1], flops=dots * d))
        reduced.append(reduce(*pieces, order=values[-1:]))

    def gather(y, order=()):
        mine = [y] + [hop(y, CORES * k) for k in steps(inner)[1:]]
        mine = call(
            functools.partial(pack_kernel, inner), shape((inner, *y.shape), bf16), mine, order=order
        )
        return mine, hop(mine, 1)

    own_probs, own_top, own_sum = call(
        own_softmax_kernel,
        (shape(piece.shape, bf16), piece, piece),
        reduced[0],
        order=(reduced[-1][0],),
    )
    probs = call(
        functools.partial(softmax_kernel, n_res - 1),
        shape((heads + 1, share, cols - r), bf16),
        (*(a for a, _ in reduced[1:]), *(b for _, b in reduced[1:]), own_top, own_sum),
    )
    own_mine, own_got = gather(own_probs, order=(probs,))
    own_part = call(
        functools.partial(own_attend_kernel, hsize),
        shape(grouped.shape, f32),
        (own_mine, own_got, values[0]),
        flops=dots * r,
    )
    mine, got = gather(probs, order=(own_part,))
    half_mix = call(
        functools.partial(half_mix_kernel, hsize, n_res - 1),
        shape((s * r, d), f32),
        (mine, *values[1:], own_part, wf),
        flops=dots * (d + cols) // 2,
    )
    return call(
        functools.partial(mix_kernel, hsize, n_res - 1),
        shape((s, r, d), bf16),
        (got, *values[1:], own_part, half_mix, wf),
        scratch=[pltpu.VMEM(x.shape, bf16), pltpu.SemaphoreType.DMA((s,))],
        flops=dots * (d + cols) // 2,
        out_space=HBM,
    )


def solution(mesh):
    n_seq, n_res = mesh.shape["seq"], mesh.shape["res"]

    def program(*args):
        return body(n_seq, n_res, *args)

    placed = (P("seq", "res", None), P(), P(), P(), P(), P())
    return jax.shard_map(
        program, mesh=mesh, in_specs=placed, out_specs=P("seq", "res", None), check_vma=False
    )
```

```python
import functools

import jax
import jax.numpy as jnp
from jax import lax
from jax.experimental import pallas as pl
from jax.experimental.pallas import tpu as pltpu
from jax.sharding import PartitionSpec as P

HEADS = 12
LANES = 128
CORES = 2

UNIT = 0.5
CODED = 80.0


VMEM = pl.BlockSpec(memory_space=pltpu.VMEM)
ANY = pl.BlockSpec(memory_space=pl.ANY)
HBM = pl.BlockSpec(memory_space=pltpu.HBM)
PARAMS = pltpu.CompilerParams(vmem_limit_bytes=48 << 20)


def spot(inner):
    place = lax.axis_index("seq")
    return place & (CORES - 1), (place >> 1) & (inner - 1)


def standardize(x, gain):
    x = x.astype(jnp.float32)
    center = x - jnp.mean(x, axis=-1, keepdims=True)
    spread = jnp.mean(center * center, axis=-1, keepdims=True)
    return (center * (1.0 / jnp.sqrt(spread + 1e-05)) * gain).astype(jnp.bfloat16)


def rows_of(x_ref, gain_ref):
    s, r, d = x_ref.shape
    return standardize(x_ref[...].reshape(s * r, d), gain_ref[...].reshape(1, d))


def project(rows, w_ref):
    return jnp.dot(rows, w_ref[...], preferred_element_type=jnp.float32).astype(jnp.bfloat16)


def lane_group(y, s, r, group):
    return jnp.concatenate(
        [y[i * r : (i + 1) * r, group * LANES : (group + 1) * LANES] for i in range(s)], axis=1
    )


def half_of(w_ref, side):
    half = w_ref.shape[1] // CORES
    return w_ref.at[:, pl.ds(pl.multiple_of(side * half, half), half)]


def write_keys(rows, w_ref, s, k_scr):
    k = project(rows, w_ref)
    for g in range(k_scr.shape[0]):
        k_scr[g] = lane_group(k, s, k_scr.shape[1], g)


def write_queries(rows, w_ref, s, hsize, q_ref):
    q = project(rows, w_ref)
    pack = LANES // hsize
    r = q_ref.shape[1] // pack
    lane = lax.broadcasted_iota(jnp.int32, (r, s * LANES), 1) % LANES // hsize
    for g in range(q_ref.shape[0]):
        both = lane_group(q, s, r, g)
        for h in range(pack):
            q_ref[g, h * r : (h + 1) * r] = jnp.where(lane == h, both, jnp.zeros_like(both))


def write_scores(q_ref, k_ref, out_ref):
    blocks, heads, share, cols = out_ref.shape
    pack = heads // q_ref.shape[0]
    r = blocks * share
    for t in range(q_ref.shape[0]):
        part = lax.dot_general(
            q_ref[t], k_ref[t], (((1,), (1,)), ((), ())), preferred_element_type=jnp.float32
        )
        for h in range(pack):
            out_ref[:, t * pack + h] = part[h * r : (h + 1) * r].reshape(blocks, share, cols)


def load(pairs, sems):
    copies = [pltpu.make_async_copy(a, b, sems.at[i]) for i, (a, b) in enumerate(pairs)]
    for copy in copies:
        copy.start()
    return copies


def own_send_kernel(
    x_hbm, gain_hbm, wk_hbm, wq_hbm,
    rows_ref, q_ref, send_ref, wk_keep_ref, wq_keep_ref,
    x_ref, gain_ref, wk_ref, wq_ref, k_scr, sems,
):
    core = spot(1)[0]
    copies = load(
        (
            (x_hbm, x_ref),
            (gain_hbm, gain_ref),
            (half_of(wk_hbm, 1 - core), wk_ref),
            (half_of(wq_hbm, 1 - core), wq_ref),
            (half_of(wk_hbm, core), wk_keep_ref),
            (half_of(wq_hbm, core), wq_keep_ref),
        ),
        sems,
    )
    s, _, d = x_ref.shape
    copies[0].wait()
    copies[1].wait()
    rows_ref[...] = rows_of(x_ref, gain_ref)
    copies[2].wait()
    write_keys(rows_ref[...], wk_ref, s, k_scr)
    copies[3].wait()
    write_queries(rows_ref[...], wq_ref, s, d // HEADS, q_ref)
    write_scores(q_ref, k_scr, send_ref)
    copies[4].wait()
    copies[5].wait()


def own_keep_kernel(rows_ref, wk_ref, wq_ref, after_ref, q_ref, keep_ref, k_scr):
    s = rows_ref.shape[0] // k_scr.shape[1]
    write_keys(rows_ref[...], wk_ref, s, k_scr)
    write_queries(rows_ref[...], wq_ref, s, rows_ref.shape[1] // HEADS, q_ref)
    write_scores(q_ref, k_scr, keep_ref)


def send_kernel(x_ref, gain_ref, wk_ref, q_ref, after_ref, rows_ref, send_ref, k_scr):
    rows_ref[...] = rows_of(x_ref, gain_ref)
    write_keys(rows_ref[...], half_of(wk_ref, 1 - spot(1)[0]), x_ref.shape[0], k_scr)
    write_scores(q_ref, k_scr, send_ref)


def keep_kernel(rows_ref, wk_ref, q_ref, after_ref, keep_ref, k_scr):
    s = rows_ref.shape[0] // k_scr.shape[1]
    write_keys(rows_ref[...], half_of(wk_ref, spot(1)[0]), s, k_scr)
    write_scores(q_ref, k_scr, keep_ref)


def write_values(rows, wv, v_ref):
    groups, r, width = v_ref.shape
    v = project(rows, wv)
    for g in range(groups):
        v_ref[g] = lane_group(v, width // LANES, r, g)


def own_value_kernel(rows_ref, wv_hbm, wf_hbm, after_ref, v_ref, wv_ref, wf_ref, sems):
    copies = load(((wv_hbm, wv_ref), (wf_hbm, wf_ref)), sems)
    copies[0].wait()
    write_values(rows_ref[...], wv_ref, v_ref)
    copies[1].wait()


def value_kernel(rows_ref, wv_ref, after_ref, v_ref):
    write_values(rows_ref[...], wv_ref, v_ref)


def encode(u):
    near = jnp.exp(jnp.clip(u, -CODED, CODED))
    far = jnp.where(u < 0, u, -1.0 / u)
    return jnp.where(jnp.abs(u) < CODED, near, far).astype(jnp.bfloat16)


def decode(y):
    y = y.astype(jnp.float32)
    near = jnp.log(jnp.abs(y))
    far = jnp.where(y < -1.0, y, -1.0 / y)
    return jnp.where(y > 0, near, far)


def steps(inner):
    return sorted(range(inner), key=lambda k: (k > 0, -k.bit_count(), k))


def merge_kernel(factor, keep_ref, got_ref, *refs):
    inner = keep_ref.shape[0]
    if refs[-1].shape == keep_ref.shape:
        outs, top_out, top_ref = refs[:-1], refs[-1], None
    else:
        outs, top_out, top_ref = refs[1:], None, refs[0]
    _, chip = spot(inner)
    for k, out_ref in zip(steps(inner), outs):
        b = chip ^ k
        u = (keep_ref[b] + got_ref[b]) * factor
        if top_out is None:
            top = top_ref[b]
        else:
            top = jnp.broadcast_to(jnp.max(u, axis=-1, keepdims=True), u.shape)
            top_out[b] = top
        u = u - top
        out_ref[...] = encode(u) if k else u


def sum_kernel(n, own_ref, *refs):
    total = own_ref[...]
    for part in refs[: n - 1]:
        total = total + decode(part[...])
    refs[-2][...] = total
    refs[-1][...] = encode(total * 0.5)


def logits_of(mine_ref, other_ref):
    return (mine_ref[...] + 2.0 * decode(other_ref[...])) * UNIT


def own_softmax_kernel(mine_ref, other_ref, after_ref, p_ref, top_ref, sum_ref):
    logits = logits_of(mine_ref, other_ref)
    top = jnp.max(logits, axis=-1, keepdims=True)
    p = jnp.exp(logits - top)
    p_ref[...] = p.astype(p_ref.dtype)
    top_ref[...] = jnp.broadcast_to(top, top_ref.shape)
    sum_ref[...] = jnp.broadcast_to(jnp.sum(p, axis=-1, keepdims=True), sum_ref.shape)


def softmax_kernel(n, *refs):
    mine, other, (own_top_ref, own_sum_ref, out_ref) = refs[:n], refs[n : 2 * n], refs[2 * n :]
    logits = jnp.concatenate([logits_of(a, b) for a, b in zip(mine, other)], axis=-1)
    heads, share, cols = logits.shape
    own_top = own_top_ref[...][..., :1]
    top = jnp.maximum(own_top, jnp.max(logits, axis=-1, keepdims=True))
    p = jnp.exp(logits - top)
    factor = jnp.exp(own_top - top)
    total = own_sum_ref[...][..., :1] * factor + jnp.sum(p, axis=-1, keepdims=True)
    out_ref[:heads] = (p / total).astype(out_ref.dtype)
    factor = factor / total
    high = factor.astype(out_ref.dtype).astype(jnp.float32)
    low = factor - high
    lane = lax.broadcasted_iota(jnp.int32, (share, cols), 1)
    packed = jnp.zeros((share, cols), jnp.float32)
    for h in range(heads):
        packed = jnp.where(lane == h, high[h], packed)
        packed = jnp.where(lane == heads + h, low[h], packed)
    out_ref[heads] = packed.astype(out_ref.dtype)


def pack_kernel(n, *refs):
    for k in range(n):
        refs[-1][k] = refs[k][...]


def weighted(p_ref, v_refs, g, t, hsize):
    pieces, _, share, _ = p_ref.shape
    pack = LANES // hsize
    r = pieces * share
    p = jnp.concatenate(
        [p_ref[:, t * pack + h].reshape(r, p_ref.shape[-1]) for h in range(pack)], axis=0
    )
    v = jnp.concatenate([v_ref[g] for v_ref in v_refs], axis=0)
    both = jnp.dot(p, v, preferred_element_type=jnp.float32)
    return pick([both[h * r : (h + 1) * r] for h in range(pack)], both.shape[1], hsize)


def pick(per_head, width, hsize):
    r = per_head[0].shape[0]
    lane = lax.broadcasted_iota(jnp.int32, (r, width), 1) % LANES // hsize
    got = jnp.broadcast_to(per_head[0], (r, width))
    for h in range(1, len(per_head)):
        got = jnp.where(lane == h, per_head[h], got)
    return got


def near(inner):
    rest = list(range(1, inner - 1))
    return list(zip(rest[::2], rest[1::2]))


def share_kernel(mine_ref, got_ref, out_ref):
    core = spot(1)[0]
    out_ref[core] = mine_ref[...]
    out_ref[1 - core] = got_ref[...]


def swap_kernel(n, *refs):
    out_ref = refs[-1]
    for j in range(n):
        out_ref[CORES * j : CORES * (j + 1)] = refs[j][...]
    out_ref[CORES * n] = refs[n][...]


def own_attend_kernel(hsize, n, share_ref, *refs):
    near_refs, (far_ref, got_ref, v_ref, out_ref, far_scr) = refs[:n], refs[n:]
    inner = CORES * n + 2
    core = spot(1)[0]
    far_scr[core] = far_ref[...]
    far_scr[1 - core] = got_ref[CORES * n]
    at = {k: j for j, k in enumerate(steps(inner))}
    blocks, places = [share_ref, far_scr], [0, at[inner - 1]]
    for j, (a, b) in enumerate(near(inner)):
        blocks += [near_refs[j], got_ref.at[CORES * j : CORES * (j + 1)]]
        places += [at[a] + core * (at[b] - at[a]), at[b] + core * (at[a] - at[b])]
    heads, share, _ = share_ref.shape[1:]
    pack = LANES // hsize
    r = share * inner
    for g in range(v_ref.shape[0]):
        side, t = divmod(g, heads // pack)
        p = jnp.concatenate(
            [block[side, t * pack + h] for h in range(pack) for block in blocks], axis=0
        )
        both = jnp.dot(p, v_ref[g], preferred_element_type=jnp.float32)
        got = pick([both[h * r : (h + 1) * r] for h in range(pack)], both.shape[1], hsize)
        for j, place in enumerate(places):
            rows = pl.ds(pl.multiple_of(place * share, share), share)
            out_ref[g, rows] = got[j * share : (j + 1) * share]


def attended(p_ref, v_refs, own_ref, side, hsize):
    pieces, heads, share, _ = p_ref.shape
    heads -= 1
    pack = LANES // hsize
    per_core = heads // pack
    width = own_ref.shape[-1]
    groups = []
    for t in range(per_core):
        g = side * per_core + t
        factors = []
        for h in range(t * pack, (t + 1) * pack):
            packed = p_ref[:, heads].reshape(pieces * share, -1).astype(jnp.float32)
            factors.append(packed[:, h : h + 1] + packed[:, heads + h : heads + h + 1])
        own = own_ref[g] * pick(factors, width, hsize)
        groups.append((own + weighted(p_ref, v_refs, g, t, hsize)).astype(jnp.bfloat16))
    return jnp.concatenate(
        [
            jnp.concatenate([g[:, i : i + LANES] for g in groups], axis=1)
            for i in range(0, width, LANES)
        ],
        axis=0,
    )


def half_rows(w_ref, side):
    half = w_ref.shape[0] // CORES
    return w_ref[pl.ds(pl.multiple_of(side * half, half), half)]


def half_mix_kernel(hsize, n, p_ref, *refs):
    v_refs, (own_ref, wf_ref, out_ref) = refs[:n], refs[n:]
    side = spot(p_ref.shape[0])[0]
    rows = attended(p_ref, v_refs, own_ref, side, hsize)
    out_ref[...] = jnp.dot(rows, half_rows(wf_ref, side), preferred_element_type=jnp.float32)


def mix_kernel(hsize, n, p_ref, *refs):
    v_refs, (own_ref, half_ref, wf_ref, out_hbm, out_ref, sems) = refs[:n], refs[n:]
    pieces = p_ref.shape[0]
    s, r, _ = out_ref.shape
    share = r // pieces
    core, chip = spot(pieces)
    rows = attended(p_ref, v_refs, own_ref, 1 - core, hsize)
    w = half_rows(wf_ref, 1 - core)
    copies = []
    for i in range(s):
        part = slice(i * r, (i + 1) * r)
        mixed = half_ref[part] + jnp.dot(rows[part], w, preferred_element_type=jnp.float32)
        mixed = mixed.astype(out_ref.dtype)
        out_ref[i] = mixed
        for n, k in enumerate(steps(pieces)):
            start = pl.multiple_of((chip ^ k) * share, share)
            copies.append(
                pltpu.make_async_copy(
                    out_ref.at[i, n * share : (n + 1) * share],
                    out_hbm.at[i, pl.ds(start, share)],
                    sems.at[i, n],
                )
            )
            copies[-1].start()
    for copy in copies:
        copy.wait()


def call(kernel, out_shape, args, order=(), hbm=(), scratch=(), flops=0, out_space=VMEM):
    ins = (*args, *(pltpu.with_memory_space_constraint(a, pltpu.HBM) for a in hbm), *order)
    specs = [VMEM] * len(args) + [HBM] * len(hbm) + [ANY] * len(order)
    moved = sum(a.size * a.dtype.itemsize for a in args)
    return pl.pallas_call(
        kernel,
        out_shape=out_shape,
        in_specs=specs,
        out_specs=jax.tree.map(lambda _: out_space, out_shape),
        scratch_shapes=list(scratch),
        compiler_params=PARAMS,
        cost_estimate=pl.CostEstimate(flops=flops, bytes_accessed=moved, transcendentals=0),
    )(*ins)


def body(n_seq, n_res, x, gain, wq, wk, wv, wf):
    s, r, d = x.shape
    groups = d // LANES
    hsize = d // HEADS
    pack = LANES // hsize
    heads = HEADS // CORES
    blocks = n_seq // CORES
    inner = blocks // 2
    share = r // inner
    cols = r * n_res
    f32, bf16 = jnp.float32, jnp.bfloat16
    shape = jax.ShapeDtypeStruct

    part = shape((inner, heads, share, r), f32)
    piece = shape((heads, share, r), f32)
    normed = shape((s * r, d), bf16)
    grouped = shape((groups, r, s * LANES), bf16)
    queries = shape((groups // CORES, pack * r, s * LANES), bf16)
    keys = pltpu.VMEM((groups // CORES, r, s * LANES), bf16)
    half = pltpu.VMEM((d, d // CORES), bf16)
    dots = 2 * s * r * d

    def hop(y, k):
        return lax.ppermute(y, "seq", [(i, i ^ k) for i in range(n_seq)])

    coded = shape((heads, share, r), bf16)
    scale = float(hsize * s * n_seq) ** -0.5
    merge = functools.partial(merge_kernel, scale / UNIT)

    def reduce(own, *sent, order=()):
        parts = [hop(y, CORES * k) for k, y in zip(steps(inner)[1:], sent)]
        total, half = call(
            functools.partial(sum_kernel, inner), (piece, coded), (own, *parts), order=order
        )
        return total, hop(half, CORES * inner)

    others = [
        lax.ppermute(x, "res", [(i, (i + k) % n_res) for i in range(n_res)])
        for k in range(1, n_res)
    ]
    kept = shape((d, d // CORES), bf16)
    rows, q_send, send, wk_keep, wq_keep = call(
        own_send_kernel,
        (normed, queries, part, kept, kept),
        (),
        hbm=(x, gain, wk, wq),
        scratch=[
            pltpu.VMEM(x.shape, bf16),
            pltpu.VMEM(gain.shape, f32),
            half,
            half,
            keys,
            pltpu.SemaphoreType.DMA((6,)),
        ],
        flops=dots * (d + r // 2),
    )
    got = hop(send, 1)
    q_keep, keep = call(
        own_keep_kernel,
        (queries, part),
        (rows, wk_keep, wq_keep),
        order=(send,),
        scratch=[keys],
        flops=dots * (d + r // 2),
    )
    *pieces, top = call(merge, (piece, *[coded] * (inner - 1), part), (keep, got))
    value, wv, wf = call(
        own_value_kernel,
        (grouped, shape(wv.shape, bf16), shape(wf.shape, bf16)),
        (rows,),
        hbm=(wv, wf),
        order=pieces[:1],
        scratch=[pltpu.SemaphoreType.DMA((2,))],
        flops=dots * d,
    )
    values = [value]
    reduced = [reduce(*pieces, order=values)]
    for other in others:
        rows, send = call(
            send_kernel,
            (normed, part),
            (other, gain, wk, q_send),
            order=(reduced[0][0],),
            scratch=[keys],
            flops=dots * (d // 2 + r // 2),
        )
        got = hop(send, 1)
        keep = call(
            keep_kernel,
            part,
            (rows, wk, q_keep),
            order=(send,),
            scratch=[keys],
            flops=dots * (d // 2 + r // 2),
        )
        pieces = call(merge, (piece, *[coded] * (inner - 1)), (keep, got, top))
        values.append(call(value_kernel, grouped, (rows, wv), order=pieces[:1], flops=dots * d))
        reduced.append(reduce(*pieces, order=values[-1:]))

    def gather(y, order=()):
        mine = [y] + [hop(y, CORES * k) for k in steps(inner)[1:]]
        mine = call(
            functools.partial(pack_kernel, inner), shape((inner, *y.shape), bf16), mine, order=order
        )
        return mine, hop(mine, 1)

    own_probs, own_top, own_sum = call(
        own_softmax_kernel,
        (shape(piece.shape, bf16), piece, piece),
        reduced[0],
        order=(reduced[-1][0],),
    )
    probs = call(
        functools.partial(softmax_kernel, n_res - 1),
        shape((heads + 1, share, cols - r), bf16),
        (*(a for a, _ in reduced[1:]), *(b for _, b in reduced[1:]), own_top, own_sum),
    )
    mate = hop(own_probs, 1)
    far = hop(own_probs, CORES * (inner - 1))
    both = call(share_kernel, shape((CORES, *own_probs.shape), bf16), (own_probs, mate))
    came = []
    for ab in near(inner):
        pairs = [(i, i ^ (CORES * ab[i % CORES])) for i in range(n_seq)]
        came.append(lax.ppermute(both, "seq", pairs))
    sent = call(
        functools.partial(swap_kernel, len(came)),
        shape((CORES * len(came) + 1, *far.shape), bf16),
        (*came, far),
        order=(probs,),
    )
    own_part = call(
        functools.partial(own_attend_kernel, hsize, len(came)),
        shape(grouped.shape, f32),
        (both, *came, far, hop(sent, 1), values[0]),
        scratch=[pltpu.VMEM(both.shape, bf16)],
        flops=dots * r,
    )
    mine, got = gather(probs, order=(own_part,))
    half_mix = call(
        functools.partial(half_mix_kernel, hsize, n_res - 1),
        shape((s * r, d), f32),
        (mine, *values[1:], own_part, wf),
        flops=dots * (d + cols) // 2,
    )
    return call(
        functools.partial(mix_kernel, hsize, n_res - 1),
        shape((s, r, d), bf16),
        (got, *values[1:], own_part, half_mix, wf),
        scratch=[pltpu.VMEM(x.shape, bf16), pltpu.SemaphoreType.DMA((s, inner))],
        flops=dots * (d + cols) // 2,
        out_space=HBM,
    )


def solution(mesh):
    n_seq, n_res = mesh.shape["seq"], mesh.shape["res"]

    def program(*args):
        return body(n_seq, n_res, *args)

    placed = (P("seq", "res", None), P(), P(), P(), P(), P())
    return jax.shard_map(
        program, mesh=mesh, in_specs=placed, out_specs=P("seq", "res", None), check_vma=False
    )
```

```python
import functools

import jax
import jax.numpy as jnp
from jax import lax
from jax.experimental import pallas as pl
from jax.experimental.pallas import tpu as pltpu
from jax.sharding import PartitionSpec as P

HEADS = 12
LANES = 128
CORES = 2

CODED = 80.0
SPREAD = 32.0
LEAST_UNIT = 0.375


VMEM = pl.BlockSpec(memory_space=pltpu.VMEM)
ANY = pl.BlockSpec(memory_space=pl.ANY)
HBM = pl.BlockSpec(memory_space=pltpu.HBM)
PARAMS = pltpu.CompilerParams(vmem_limit_bytes=48 << 20)


def spot(inner):
    place = lax.axis_index("seq")
    return place & (CORES - 1), (place >> 1) & (inner - 1)


def standardize(x, gain):
    x = x.astype(jnp.float32)
    center = x - jnp.mean(x, axis=-1, keepdims=True)
    spread = jnp.mean(center * center, axis=-1, keepdims=True)
    return (center * (1.0 / jnp.sqrt(spread + 1e-05)) * gain).astype(jnp.bfloat16)


def rows_of(x_ref, gain_ref):
    s, r, d = x_ref.shape
    return standardize(x_ref[...].reshape(s * r, d), gain_ref[...].reshape(1, d))


def project(rows, w_ref):
    return jnp.dot(rows, w_ref[...], preferred_element_type=jnp.float32).astype(jnp.bfloat16)


def lane_group(y, s, r, group):
    return jnp.concatenate(
        [y[i * r : (i + 1) * r, group * LANES : (group + 1) * LANES] for i in range(s)], axis=1
    )


def half_of(w_ref, side):
    half = w_ref.shape[1] // CORES
    return w_ref.at[:, pl.ds(pl.multiple_of(side * half, half), half)]


def write_keys(rows, w_ref, s, k_scr):
    k = project(rows, w_ref)
    for g in range(k_scr.shape[0]):
        k_scr[g] = lane_group(k, s, k_scr.shape[1], g)


def write_queries(rows, w_ref, s, hsize, q_ref):
    q = project(rows, w_ref)
    pack = LANES // hsize
    r = q_ref.shape[1] // pack
    lane = lax.broadcasted_iota(jnp.int32, (r, s * LANES), 1) % LANES // hsize
    for g in range(q_ref.shape[0]):
        both = lane_group(q, s, r, g)
        for h in range(pack):
            q_ref[g, h * r : (h + 1) * r] = jnp.where(lane == h, both, jnp.zeros_like(both))


def write_scores(q_ref, k_ref, out_ref):
    blocks, heads, share, cols = out_ref.shape
    pack = heads // q_ref.shape[0]
    r = blocks * share
    for t in range(q_ref.shape[0]):
        part = lax.dot_general(
            q_ref[t], k_ref[t], (((1,), (1,)), ((), ())), preferred_element_type=jnp.float32
        )
        for h in range(pack):
            out_ref[:, t * pack + h] = part[h * r : (h + 1) * r].reshape(blocks, share, cols)


def load(pairs, sems):
    copies = [pltpu.make_async_copy(a, b, sems.at[i]) for i, (a, b) in enumerate(pairs)]
    for copy in copies:
        copy.start()
    return copies


def own_send_kernel(
    x_hbm, gain_hbm, wk_hbm, wq_hbm,
    rows_ref, q_ref, send_ref, wk_keep_ref, wq_keep_ref,
    x_ref, gain_ref, wk_ref, wq_ref, k_scr, sems,
):
    core = spot(1)[0]
    copies = load(
        (
            (x_hbm, x_ref),
            (gain_hbm, gain_ref),
            (half_of(wk_hbm, 1 - core), wk_ref),
            (half_of(wq_hbm, 1 - core), wq_ref),
            (half_of(wk_hbm, core), wk_keep_ref),
            (half_of(wq_hbm, core), wq_keep_ref),
        ),
        sems,
    )
    s, _, d = x_ref.shape
    copies[0].wait()
    copies[1].wait()
    rows_ref[...] = rows_of(x_ref, gain_ref)
    copies[2].wait()
    write_keys(rows_ref[...], wk_ref, s, k_scr)
    copies[3].wait()
    write_queries(rows_ref[...], wq_ref, s, d // HEADS, q_ref)
    write_scores(q_ref, k_scr, send_ref)
    copies[4].wait()
    copies[5].wait()


def own_keep_kernel(rows_ref, wk_ref, wq_ref, after_ref, q_ref, keep_ref, k_scr):
    s = rows_ref.shape[0] // k_scr.shape[1]
    write_keys(rows_ref[...], wk_ref, s, k_scr)
    write_queries(rows_ref[...], wq_ref, s, rows_ref.shape[1] // HEADS, q_ref)
    write_scores(q_ref, k_scr, keep_ref)


def send_kernel(x_ref, gain_ref, wk_ref, q_ref, after_ref, rows_ref, send_ref, k_scr):
    rows_ref[...] = rows_of(x_ref, gain_ref)
    write_keys(rows_ref[...], half_of(wk_ref, 1 - spot(1)[0]), x_ref.shape[0], k_scr)
    write_scores(q_ref, k_scr, send_ref)


def keep_kernel(rows_ref, wk_ref, q_ref, after_ref, keep_ref, k_scr):
    s = rows_ref.shape[0] // k_scr.shape[1]
    write_keys(rows_ref[...], half_of(wk_ref, spot(1)[0]), s, k_scr)
    write_scores(q_ref, k_scr, keep_ref)


def write_values(rows, wv, v_ref):
    groups, r, width = v_ref.shape
    v = project(rows, wv)
    for g in range(groups):
        v_ref[g] = lane_group(v, width // LANES, r, g)


def own_value_kernel(rows_ref, wv_hbm, wf_hbm, after_ref, v_ref, wv_ref, wf_ref, sems):
    copies = load(((wv_hbm, wv_ref), (wf_hbm, wf_ref)), sems)
    copies[0].wait()
    write_values(rows_ref[...], wv_ref, v_ref)
    copies[1].wait()


def value_kernel(rows_ref, wv_ref, after_ref, v_ref):
    write_values(rows_ref[...], wv_ref, v_ref)


def encode(u):
    near = jnp.exp(jnp.clip(u, -CODED, CODED))
    far = jnp.where(u < 0, u, -1.0 / u)
    return jnp.where(jnp.abs(u) < CODED, near, far).astype(jnp.bfloat16)


def reference_of(v):
    top = jnp.max(v, axis=-1, keepdims=True)
    spread = top - jnp.min(v, axis=-1, keepdims=True)
    unit = jnp.maximum(spread * (1.0 / SPREAD), LEAST_UNIT)
    return top, unit.astype(jnp.bfloat16).astype(jnp.float32)


def write_with_units(out_ref, v, unit):
    heads, share, cols = v.shape
    out_ref[:heads] = encode(v * (1.0 / unit))
    lane = lax.broadcasted_iota(jnp.int32, (share, cols), 1)
    packed = jnp.zeros((share, cols), jnp.float32)
    for h in range(heads):
        packed = jnp.where(lane == h, unit[h], packed)
    out_ref[heads] = packed.astype(out_ref.dtype)


def write_units(part_ref, unit_ref):
    heads, share, cols = unit_ref.shape
    packed = part_ref[heads].astype(jnp.float32)
    for h in range(heads):
        unit_ref[h] = jnp.broadcast_to(packed[:, h : h + 1], (share, cols))


def decode(y):
    y = y.astype(jnp.float32)
    near = jnp.log(jnp.abs(y))
    far = jnp.where(y < -1.0, y, -1.0 / y)
    return jnp.where(y > 0, near, far)


def steps(inner):
    return sorted(range(inner), key=lambda k: (k > 0, -k.bit_count(), k))


def own_merge_kernel(scale, keep_ref, got_ref, *refs):
    inner = keep_ref.shape[0]
    outs, top_ref, inverse_ref = refs[:inner], refs[inner], refs[inner + 1]
    _, chip = spot(inner)
    for k, out_ref in zip(steps(inner), outs):
        b = chip ^ k
        v = (keep_ref[b] + got_ref[b]) * scale
        top, unit = reference_of(v)
        top_ref[b] = jnp.broadcast_to(top, v.shape)
        inverse_ref[b] = jnp.broadcast_to(1.0 / unit, v.shape)
        if k:
            write_with_units(out_ref, v - top, unit)
        else:
            out_ref[...] = v - top


def merge_kernel(scale, keep_ref, got_ref, top_ref, inverse_ref, *outs):
    inner = keep_ref.shape[0]
    _, chip = spot(inner)
    for k, out_ref in zip(steps(inner), outs):
        b = chip ^ k
        v = (keep_ref[b] + got_ref[b]) * scale - top_ref[b]
        out_ref[...] = encode(v * inverse_ref[b]) if k else v


def own_sum_kernel(n, own_ref, *refs):
    parts, outs = refs[: n - 1], refs[-(n + 3) :]
    total_ref, sent_ref, top_ref, inverse_ref, *unit_refs = outs
    total = own_ref[...]
    for part_ref, unit_ref in zip(parts, unit_refs):
        write_units(part_ref, unit_ref)
        total = total + unit_ref[...] * decode(part_ref[: total.shape[0]])
    top, unit = reference_of(total)
    total = total - top
    total_ref[...] = total
    write_with_units(sent_ref, total, unit)
    top_ref[...] = jnp.broadcast_to(top, total.shape)
    inverse_ref[...] = jnp.broadcast_to(1.0 / unit, total.shape)


def sum_kernel(n, own_ref, *refs):
    parts, (top_ref, inverse_ref, *unit_refs) = refs[: n - 1], refs[n - 1 : 2 * n]
    total_ref, sent_ref = refs[-2:]
    total = own_ref[...] - top_ref[...]
    for part_ref, unit_ref in zip(parts, unit_refs):
        total = total + unit_ref[...] * decode(part_ref[...])
    total_ref[...] = total
    sent_ref[...] = encode(total * inverse_ref[...])


def own_softmax_kernel(mine_ref, other_ref, after_ref, p_ref, top_ref, sum_ref, unit_ref):
    write_units(other_ref, unit_ref)
    logits = mine_ref[...] + unit_ref[...] * decode(other_ref[: mine_ref.shape[0]])
    top = jnp.max(logits, axis=-1, keepdims=True)
    p = jnp.exp(logits - top)
    p_ref[...] = p.astype(p_ref.dtype)
    top_ref[...] = jnp.broadcast_to(top, top_ref.shape)
    sum_ref[...] = jnp.broadcast_to(jnp.sum(p, axis=-1, keepdims=True), sum_ref.shape)


def softmax_kernel(n, *refs):
    mine, other = refs[:n], refs[n : 2 * n]
    own_top_ref, own_sum_ref, unit_ref, out_ref = refs[2 * n :]
    logits = jnp.concatenate(
        [a[...] + unit_ref[...] * decode(b[...]) for a, b in zip(mine, other)], axis=-1
    )
    heads, share, cols = logits.shape
    own_top = own_top_ref[...][..., :1]
    top = jnp.maximum(own_top, jnp.max(logits, axis=-1, keepdims=True))
    p = jnp.exp(logits - top)
    factor = jnp.exp(own_top - top)
    total = own_sum_ref[...][..., :1] * factor + jnp.sum(p, axis=-1, keepdims=True)
    share_of = 1.0 / total
    out_ref[:heads] = (p * share_of).astype(out_ref.dtype)
    factor = factor * share_of
    high = factor.astype(out_ref.dtype).astype(jnp.float32)
    low = factor - high
    lane = lax.broadcasted_iota(jnp.int32, (share, cols), 1)
    packed = jnp.zeros((share, cols), jnp.float32)
    for h in range(heads):
        packed = jnp.where(lane == h, high[h], packed)
        packed = jnp.where(lane == heads + h, low[h], packed)
    out_ref[heads] = packed.astype(out_ref.dtype)


def pack_kernel(n, *refs):
    for k in range(n):
        refs[-1][k] = refs[k][...]


def weighted(p_ref, v_refs, g, t, hsize):
    pieces, _, share, _ = p_ref.shape
    pack = LANES // hsize
    r = pieces * share
    p = jnp.concatenate(
        [p_ref[:, t * pack + h].reshape(r, p_ref.shape[-1]) for h in range(pack)], axis=0
    )
    v = jnp.concatenate([v_ref[g] for v_ref in v_refs], axis=0)
    both = jnp.dot(p, v, preferred_element_type=jnp.float32)
    return pick([both[h * r : (h + 1) * r] for h in range(pack)], both.shape[1], hsize)


def pick(per_head, width, hsize):
    r = per_head[0].shape[0]
    lane = lax.broadcasted_iota(jnp.int32, (r, width), 1) % LANES // hsize
    got = jnp.broadcast_to(per_head[0], (r, width))
    for h in range(1, len(per_head)):
        got = jnp.where(lane == h, per_head[h], got)
    return got


def near(inner):
    rest = list(range(1, inner - 1))
    return list(zip(rest[::2], rest[1::2]))


def share_kernel(mine_ref, got_ref, out_ref):
    core = spot(1)[0]
    out_ref[core] = mine_ref[...]
    out_ref[1 - core] = got_ref[...]


def swap_kernel(n, *refs):
    out_ref = refs[-1]
    for j in range(n):
        out_ref[CORES * j : CORES * (j + 1)] = refs[j][...]
    out_ref[CORES * n] = refs[n][...]


def own_attend_kernel(hsize, n, share_ref, *refs):
    near_refs, (far_ref, got_ref, v_ref, out_ref, far_scr) = refs[:n], refs[n:]
    inner = CORES * n + 2
    core = spot(1)[0]
    far_scr[core] = far_ref[...]
    far_scr[1 - core] = got_ref[CORES * n]
    at = {k: j for j, k in enumerate(steps(inner))}
    blocks, places = [share_ref, far_scr], [0, at[inner - 1]]
    for j, (a, b) in enumerate(near(inner)):
        blocks += [near_refs[j], got_ref.at[CORES * j : CORES * (j + 1)]]
        places += [at[a] + core * (at[b] - at[a]), at[b] + core * (at[a] - at[b])]
    heads, share, _ = share_ref.shape[1:]
    pack = LANES // hsize
    r = share * inner
    for g in range(v_ref.shape[0]):
        side, t = divmod(g, heads // pack)
        p = jnp.concatenate(
            [block[side, t * pack + h] for h in range(pack) for block in blocks], axis=0
        )
        both = jnp.dot(p, v_ref[g], preferred_element_type=jnp.float32)
        got = pick([both[h * r : (h + 1) * r] for h in range(pack)], both.shape[1], hsize)
        for j, place in enumerate(places):
            rows = pl.ds(pl.multiple_of(place * share, share), share)
            out_ref[g, rows] = got[j * share : (j + 1) * share]


def attended(p_ref, v_refs, own_ref, side, hsize):
    pieces, heads, share, _ = p_ref.shape
    heads -= 1
    pack = LANES // hsize
    per_core = heads // pack
    width = own_ref.shape[-1]
    groups = []
    for t in range(per_core):
        g = side * per_core + t
        factors = []
        for h in range(t * pack, (t + 1) * pack):
            packed = p_ref[:, heads].reshape(pieces * share, -1).astype(jnp.float32)
            factors.append(packed[:, h : h + 1] + packed[:, heads + h : heads + h + 1])
        own = own_ref[g] * pick(factors, width, hsize)
        groups.append((own + weighted(p_ref, v_refs, g, t, hsize)).astype(jnp.bfloat16))
    return jnp.concatenate(
        [
            jnp.concatenate([g[:, i : i + LANES] for g in groups], axis=1)
            for i in range(0, width, LANES)
        ],
        axis=0,
    )


def half_rows(w_ref, side):
    half = w_ref.shape[0] // CORES
    return w_ref[pl.ds(pl.multiple_of(side * half, half), half)]


def half_mix_kernel(hsize, n, p_ref, *refs):
    v_refs, (own_ref, wf_ref, out_ref) = refs[:n], refs[n:]
    side = spot(p_ref.shape[0])[0]
    rows = attended(p_ref, v_refs, own_ref, side, hsize)
    out_ref[...] = jnp.dot(rows, half_rows(wf_ref, side), preferred_element_type=jnp.float32)


def mix_kernel(hsize, n, p_ref, *refs):
    v_refs, (own_ref, half_ref, wf_ref, out_hbm, out_ref, sems) = refs[:n], refs[n:]
    pieces = p_ref.shape[0]
    s, r, _ = out_ref.shape
    share = r // pieces
    core, chip = spot(pieces)
    rows = attended(p_ref, v_refs, own_ref, 1 - core, hsize)
    w = half_rows(wf_ref, 1 - core)
    copies = []
    for i in range(s):
        part = slice(i * r, (i + 1) * r)
        mixed = half_ref[part] + jnp.dot(rows[part], w, preferred_element_type=jnp.float32)
        mixed = mixed.astype(out_ref.dtype)
        out_ref[i] = mixed
        for n, k in enumerate(steps(pieces)):
            start = pl.multiple_of((chip ^ k) * share, share)
            copies.append(
                pltpu.make_async_copy(
                    out_ref.at[i, n * share : (n + 1) * share],
                    out_hbm.at[i, pl.ds(start, share)],
                    sems.at[i, n],
                )
            )
            copies[-1].start()
    for copy in copies:
        copy.wait()


def call(kernel, out_shape, args, order=(), hbm=(), scratch=(), flops=0, out_space=VMEM):
    ins = (*args, *(pltpu.with_memory_space_constraint(a, pltpu.HBM) for a in hbm), *order)
    specs = [VMEM] * len(args) + [HBM] * len(hbm) + [ANY] * len(order)
    moved = sum(a.size * a.dtype.itemsize for a in args)
    return pl.pallas_call(
        kernel,
        out_shape=out_shape,
        in_specs=specs,
        out_specs=jax.tree.map(lambda _: out_space, out_shape),
        scratch_shapes=list(scratch),
        compiler_params=PARAMS,
        cost_estimate=pl.CostEstimate(flops=flops, bytes_accessed=moved, transcendentals=0),
    )(*ins)


def body(n_seq, n_res, x, gain, wq, wk, wv, wf):
    s, r, d = x.shape
    groups = d // LANES
    hsize = d // HEADS
    pack = LANES // hsize
    heads = HEADS // CORES
    blocks = n_seq // CORES
    inner = blocks // 2
    share = r // inner
    cols = r * n_res
    f32, bf16 = jnp.float32, jnp.bfloat16
    shape = jax.ShapeDtypeStruct

    part = shape((inner, heads, share, r), f32)
    piece = shape((heads, share, r), f32)
    normed = shape((s * r, d), bf16)
    grouped = shape((groups, r, s * LANES), bf16)
    queries = shape((groups // CORES, pack * r, s * LANES), bf16)
    keys = pltpu.VMEM((groups // CORES, r, s * LANES), bf16)
    half = pltpu.VMEM((d, d // CORES), bf16)
    dots = 2 * s * r * d

    def hop(y, k):
        return lax.ppermute(y, "seq", [(i, i ^ k) for i in range(n_seq)])

    coded = shape((heads, share, r), bf16)
    scale = float(hsize * s * n_seq) ** -0.5
    united = shape((heads + 1, share, r), bf16)

    def quad(sent):
        return [hop(y, CORES * k) for k, y in zip(steps(inner)[1:], sent)]

    others = [
        lax.ppermute(x, "res", [(i, (i + k) % n_res) for i in range(n_res)])
        for k in range(1, n_res)
    ]
    kept = shape((d, d // CORES), bf16)
    rows, q_send, send, wk_keep, wq_keep = call(
        own_send_kernel,
        (normed, queries, part, kept, kept),
        (),
        hbm=(x, gain, wk, wq),
        scratch=[
            pltpu.VMEM(x.shape, bf16),
            pltpu.VMEM(gain.shape, f32),
            half,
            half,
            keys,
            pltpu.SemaphoreType.DMA((6,)),
        ],
        flops=dots * (d + r // 2),
    )
    got = hop(send, 1)
    q_keep, keep = call(
        own_keep_kernel,
        (queries, part),
        (rows, wk_keep, wq_keep),
        order=(send,),
        scratch=[keys],
        flops=dots * (d + r // 2),
    )
    *pieces, top, inverse = call(
        functools.partial(own_merge_kernel, scale),
        (piece, *[united] * (inner - 1), part, part),
        (keep, got),
    )
    value, wv, wf = call(
        own_value_kernel,
        (grouped, shape(wv.shape, bf16), shape(wf.shape, bf16)),
        (rows,),
        hbm=(wv, wf),
        order=pieces[:1],
        scratch=[pltpu.SemaphoreType.DMA((2,))],
        flops=dots * d,
    )
    values = [value]
    total, half, *known = call(
        functools.partial(own_sum_kernel, inner),
        (piece, united, *[piece] * (inner + 1)),
        (pieces[0], *quad(pieces[1:])),
        order=values,
    )
    reduced = [(total, hop(half, CORES * inner))]
    for other in others:
        rows, send = call(
            send_kernel,
            (normed, part),
            (other, gain, wk, q_send),
            order=(reduced[0][0],),
            scratch=[keys],
            flops=dots * (d // 2 + r // 2),
        )
        got = hop(send, 1)
        keep = call(
            keep_kernel,
            part,
            (rows, wk, q_keep),
            order=(send,),
            scratch=[keys],
            flops=dots * (d // 2 + r // 2),
        )
        pieces = call(
            functools.partial(merge_kernel, scale),
            (piece, *[coded] * (inner - 1)),
            (keep, got, top, inverse),
        )
        values.append(call(value_kernel, grouped, (rows, wv), order=pieces[:1], flops=dots * d))
        total, half = call(
            functools.partial(sum_kernel, inner),
            (piece, coded),
            (pieces[0], *quad(pieces[1:]), *known),
            order=values[-1:],
        )
        reduced.append((total, hop(half, CORES * inner)))

    def gather(y, order=()):
        mine = [y] + [hop(y, CORES * k) for k in steps(inner)[1:]]
        mine = call(
            functools.partial(pack_kernel, inner), shape((inner, *y.shape), bf16), mine, order=order
        )
        return mine, hop(mine, 1)

    own_probs, own_top, own_sum, own_unit = call(
        own_softmax_kernel,
        (shape(piece.shape, bf16), piece, piece, piece),
        reduced[0],
        order=(reduced[-1][0],),
    )
    probs = call(
        functools.partial(softmax_kernel, n_res - 1),
        shape((heads + 1, share, cols - r), bf16),
        (*(a for a, _ in reduced[1:]), *(b for _, b in reduced[1:]), own_top, own_sum, own_unit),
    )
    mate = hop(own_probs, 1)
    far = hop(own_probs, CORES * (inner - 1))
    both = call(share_kernel, shape((CORES, *own_probs.shape), bf16), (own_probs, mate))
    came = []
    for ab in near(inner):
        pairs = [(i, i ^ (CORES * ab[i % CORES])) for i in range(n_seq)]
        came.append(lax.ppermute(both, "seq", pairs))
    sent = call(
        functools.partial(swap_kernel, len(came)),
        shape((CORES * len(came) + 1, *far.shape), bf16),
        (*came, far),
        order=(probs,),
    )
    own_part = call(
        functools.partial(own_attend_kernel, hsize, len(came)),
        shape(grouped.shape, f32),
        (both, *came, far, hop(sent, 1), values[0]),
        scratch=[pltpu.VMEM(both.shape, bf16)],
        flops=dots * r,
    )
    mine, got = gather(probs, order=(own_part,))
    half_mix = call(
        functools.partial(half_mix_kernel, hsize, n_res - 1),
        shape((s * r, d), f32),
        (mine, *values[1:], own_part, wf),
        flops=dots * (d + cols) // 2,
    )
    return call(
        functools.partial(mix_kernel, hsize, n_res - 1),
        shape((s, r, d), bf16),
        (got, *values[1:], own_part, half_mix, wf),
        scratch=[pltpu.VMEM(x.shape, bf16), pltpu.SemaphoreType.DMA((s, inner))],
        flops=dots * (d + cols) // 2,
        out_space=HBM,
    )


def solution(mesh):
    n_seq, n_res = mesh.shape["seq"], mesh.shape["res"]

    def program(*args):
        return body(n_seq, n_res, *args)

    placed = (P("seq", "res", None), P(), P(), P(), P(), P())
    return jax.shard_map(
        program, mesh=mesh, in_specs=placed, out_specs=P("seq", "res", None), check_vma=False
    )
```
